32 devices in a mesh: groups: 2 (over x), ctx: 16 (over z, y, core).
Axes of the slice: x: 2, y: 2, z: 4, core: 2. Of those that a mesh axis runs over, the one named last changes fastest.
Arguments:
- queries: bfloat16 [4096, 2048], P(('groups', 'ctx')), parts along dimension 0, may hold values from -64 to 64
- keys: bfloat16 [4096, 512], P(('groups', 'ctx')), parts along dimension 0, may hold values from -6 to 6
- values: bfloat16 [4096, 512], P(('groups', 'ctx')), parts along dimension 0, may hold values from -6 to 6
- block_ids: int32 [4096], P(('groups', 'ctx')), parts along dimension 0, may hold values from 0 to 3, as said below
- out_weight: bfloat16 [2048, 2048], P('ctx'), may hold values from -0.59765625 to 0.59765625
- summary_gain: float32 [128], replicated, may hold values from 0.1 to 1.9
- norm_gain: float32 [2048], replicated, may hold values from 0.1 to 1.9
- routes: int32 [4096, 8], P(('groups', 'ctx')), parts along dimension 0, may hold values from 0 to 15, all different within a row; in each aligned block of 128 rows (0 to 127, 128 to 255, ...) at most 80 rows name the same one
- route_scores: float32 [4096, 8], P(('groups', 'ctx')), parts along dimension 0, may hold values from 0.02 to 1
- expert_gate: bfloat16 [16, 2048, 768], P('ctx'), may hold values from -0.125 to 0.125
- expert_up: bfloat16 [16, 2048, 768], P('ctx'), may hold values from -0.125 to 0.125
- expert_down: bfloat16 [16, 768, 2048], P('ctx'), may hold values from -0.21875 to 0.21875
Outputs:
- projected: bfloat16 [4096, 2048], P(('groups', 'ctx')), parts along dimension 0
- mixed: bfloat16 [4096, 2048], P(('groups', 'ctx')), parts along dimension 0
The draws below stay inside these ranges and needn't reach their ends.
There are 2 independent parts, one for each index of `groups`. The reference program is written for one: setup_inputs(seed, part) draws one part's arguments, and reference() takes and returns one part's arrays. A program takes and returns all parts, laid end to end along the dimension named above; an argument that names none is the same for every part. Nothing has to cross between parts.
Inputs may be any that keep to these rules, and one draw needn't show every extreme that they name: `block_ids`: within each context shard's 128 tokens the block numbers never fall, start at 0 and take every value up to 3. `routes`: among the 128 tokens of one context shard no expert is chosen more than 80 times, and in every draw some expert is chosen exactly 80 times by some shard. A token's 8 experts differ.
All inputs are finite; a program needn't handle non-finite values.
Results may differ from the reference program's by a relative error of at most 0.0077.
Values may be sent and summed in bfloat16 or wider, within the bound.
A program may use at most 128 MiB of HBM per device.

```python
import math
import jax
import jax.numpy as jnp
import numpy as np
from jax import lax

D = 2048
HQ = 16
KVH = 4
HD = 128
FF = 768
TOP = 8
NB = 4
TOK_DEV = 128
TOKENS = 2048
EXPERTS = 16
CAP = 80


def query_key_pair(key):
    key_q = jax.random.fold_in(key, 101)
    key_k = jax.random.fold_in(key, 202)
    query = jax.random.truncated_normal(key_q, -6.0, 6.0, (TOKENS, HQ * HD), jnp.float32)
    keyed = jax.random.truncated_normal(key_k, -6.0, 6.0, (TOKENS, KVH * HD), jnp.float32)
    return (query, keyed)


def draw_queries(key, part):
    return query_key_pair(key)[0].astype(jnp.bfloat16)


def draw_keys(key, part):
    return query_key_pair(key)[1].astype(jnp.bfloat16)


def draw_block_ids(key, part):
    shards = TOKENS // TOK_DEV
    subkeys = jax.random.split(jax.random.fold_in(key, 303), shards)

    def one_shard(sub):
        cuts = jax.random.permutation(sub, TOK_DEV - 1)[:NB - 1] + 1
        position = jnp.arange(TOK_DEV)
        return jnp.sum((position[:, None] >= cuts[None, :]).astype(jnp.int32), axis=-1)
    return jax.vmap(one_shard)(subkeys).reshape(TOKENS).astype(jnp.int32)


def level_of(rng, shape, cuts, smallest, top_value):
    level = 1.0
    for dim, parts in cuts:
        heights = jax.random.uniform(jax.random.fold_in(jax.random.fold_in(rng, 6), dim), (parts,), jnp.float32, smallest / len(cuts), top_value / len(cuts))
        level = level * jnp.repeat(jnp.exp(heights), shape[dim] // parts).reshape((-1,) + (1,) * (len(shape) - 1 - dim))
    return level


def deal_out(stream_key, own, number, rows, number_of, top, most, slope):
    order = jax.random.permutation(stream_key, number_of)
    crowded, common = portions_of(number_of, rows * top, most, slope, True), portions_of(number_of, rows * top, most, slope, False)
    places = jnp.arange(number_of)

    def named(lengths, turn):
        used = int((lengths > 0).sum())
        fixed = max(1, used // 4)
        moved = fixed + (places - fixed + turn * (used - fixed)) % max(1, number_of - fixed)
        return jnp.zeros((number_of,), jnp.int32).at[order[jnp.where(places < fixed, places, moved)]].set(jnp.asarray(lengths, jnp.int32))

    lengths = jnp.where(number % 4 == 0, named(crowded, number // 4), named(common, number - number // 4 - 1))
    mixed = jax.random.permutation(jax.random.fold_in(own, 3), number_of)
    giver, sink = mixed[0:number_of // 2 * 2:2], mixed[1:number_of // 2 * 2:2]
    room = jnp.minimum(lengths[giver] - 1, most - lengths[sink]) // 2
    room = jnp.where((giver == order[0]) | (sink == order[0]) | (lengths[sink] == 0), 0, jnp.maximum(room, 0))
    moved = jax.random.randint(jax.random.fold_in(own, 4), (number_of // 2,), 0, 1 << 20) % (room + 1)
    lengths = lengths.at[giver].add(-moved).at[sink].add(moved)
    members = jnp.searchsorted(jnp.cumsum(lengths), jnp.arange(rows * top), side="right").astype(jnp.int32)
    listing = members.reshape(top, rows).T
    listing = listing[jax.random.permutation(jax.random.fold_in(own, 1), rows)]
    turn = jax.random.randint(jax.random.fold_in(own, 2), (rows, 1), 0, top)
    return jnp.take_along_axis(listing, (jnp.arange(top)[None, :] + turn) % top, axis=1)


def portions_of(count, total, limit, lean, full):
    portions = [(1 << 20) // math.isqrt(rank ** lean) + 1 for rank in range(1, count + 1)]
    largest = limit if full else min(limit, max(-(-total // count), total * portions[0] // sum(portions)))
    least = 1 if total - largest >= count - 1 else 0
    holding, spare = [largest] + [least] * (count - 1), total - largest - least * (count - 1)
    while spare > 0:
        free = [i for i in range(1, count) if holding[i] < largest] or [i for i in range(1, count) if holding[i] < limit]
        mass, budget = sum([portions[i] for i in free]), spare
        for i in free:
            more = min(limit - holding[i], max(1, budget * portions[i] // mass), spare)
            holding[i] = holding[i] + more
            spare = spare - more
    return np.array(holding)


def scatter_about(own_key, dims, spread, limit, pieces=(), held_as=jnp.bfloat16):
    array = jax.random.normal(own_key, dims, jnp.float32) * spread
    if len(pieces) > 0:
        array = level_of(own_key, dims, pieces, -0.22, 0.18) * array
    return jnp.clip(array, min=-limit, max=limit).astype(held_as)


def setup_inputs(seed: int = 0, part: int = 0) -> dict:
    seeds = jax.random.split(jax.random.key(seed), 13)
    part_splits = jax.random.split(jax.random.fold_in(seeds[12], part), 13)
    queries = draw_queries(jax.random.fold_in(jax.random.fold_in(seeds[12], part), 71), part)
    keys = draw_keys(jax.random.fold_in(jax.random.fold_in(seeds[12], part), 71), part)
    values = scatter_about(part_splits[2], (TOKENS, KVH * HD), 1.0, 6.0, ((0, 16),))
    block_ids = draw_block_ids(jax.random.fold_in(jax.random.fold_in(seeds[12], part), 71), part)
    out_weight = scatter_about(seeds[4], (HQ * HD, D), 0.1, 0.59765625, ((0, 16),))
    summary_gain = jnp.clip(1.0 + 0.18 * jax.random.normal(seeds[5], (HD,), jnp.float32), 0.1, 1.9)
    norm_gain = jnp.clip(1.0 + 0.18 * jax.random.normal(seeds[6], (D,), jnp.float32), 0.1, 1.9)
    routes_keys = jax.random.split(jax.random.fold_in(part_splits[7], 1), TOKENS // TOK_DEV)
    routes_turns = jax.random.permutation(jax.random.fold_in(part_splits[7], 3), TOKENS // TOK_DEV)
    routes = jax.vmap(lambda own, number: deal_out(jax.random.fold_in(part_splits[7], 2), own, number, TOK_DEV, EXPERTS, TOP, CAP, 2))(routes_keys, routes_turns).reshape((TOKENS, TOP))
    route_scores = jnp.clip(jnp.exp(math.log(1.0) - 3.912023 * jax.random.uniform(part_splits[8], (TOKENS, TOP), jnp.float32) ** level_of(part_splits[8], (TOKENS, TOP), ((0, 16),), -0.2, 0.2)), 0.02, 1.0)
    expert_gate = scatter_about(seeds[9], (EXPERTS, D, FF), D ** -0.5, 0.125, ((0, 16),))
    expert_up = scatter_about(seeds[10], (EXPERTS, D, FF), D ** -0.5, 0.125, ((0, 16),))
    expert_down = scatter_about(seeds[11], (EXPERTS, FF, D), FF ** -0.5, 0.21875, ((0, 16),))
    return {"queries": queries, "keys": keys, "values": values, "block_ids": block_ids, "out_weight": out_weight, "summary_gain": summary_gain, "norm_gain": norm_gain, "routes": routes, "route_scores": route_scores, "expert_gate": expert_gate, "expert_up": expert_up, "expert_down": expert_down}


def normalize(x):
    return x * lax.rsqrt(lax.optimization_barrier(jnp.mean(x * x, axis=-1, keepdims=True)) + 1e-06)

def reference(queries, keys, values, block_ids, out_weight, summary_gain, norm_gain, routes, route_scores, expert_gate, expert_up, expert_down):
    shards = TOKENS // TOK_DEV
    group = HQ // KVH
    scale = 1.0 / math.sqrt(HD)
    keys4 = keys.astype(jnp.float32).reshape(shards, TOK_DEV, KVH, HD)
    values4 = values.astype(jnp.float32).reshape(shards, TOK_DEV, KVH, HD)
    blocks = block_ids.reshape(shards, TOK_DEV)
    member = (blocks[:, None, :] == jnp.arange(NB, dtype=jnp.int32)[None, :, None]).astype(jnp.float32)
    count = lax.optimization_barrier(jnp.sum(member, axis=-1))
    kmean = jnp.einsum('nbt,ntkd->nbkd', member, keys4) / count[:, :, None, None]
    vmean = jnp.einsum('nbt,ntkd->nbkd', member, values4) / count[:, :, None, None]
    summary_keys = (normalize(kmean) * summary_gain.astype(jnp.float32)).astype(jnp.bfloat16).reshape(shards * NB, KVH, HD)
    summary_values = normalize(vmean).astype(jnp.bfloat16).reshape(shards * NB, KVH, HD)
    owner = jnp.arange(shards * NB, dtype=jnp.int32) // NB
    causal = jnp.arange(TOK_DEV)[:, None] >= jnp.arange(TOK_DEV)[None, :]

    def attend(index):
        start = (index * TOK_DEV).astype(jnp.int32)
        query = lax.dynamic_slice_in_dim(queries, start, TOK_DEV, 0).astype(jnp.float32).reshape(TOK_DEV, KVH, group, HD)
        key_loc = lax.dynamic_slice_in_dim(keys, start, TOK_DEV, 0).astype(jnp.float32).reshape(TOK_DEV, KVH, HD)
        val_loc = lax.dynamic_slice_in_dim(values, start, TOK_DEV, 0).reshape(TOK_DEV, KVH, HD)
        local = jnp.einsum('tkgd,skd->kgts', query, key_loc) * scale
        local = jnp.where(causal[None, None], local, -jnp.inf)
        remote = jnp.einsum('tkgd,skd->kgts', query, summary_keys.astype(jnp.float32)) * scale
        remote = jnp.where((owner < index)[None, None, None, :], remote, -jnp.inf)
        scores = jnp.concatenate([local, remote], axis=-1)
        top = lax.optimization_barrier(jnp.max(scores, axis=-1, keepdims=True))
        expo = jnp.exp(scores - top)
        weights = (expo / lax.optimization_barrier(jnp.sum(expo, axis=-1, keepdims=True))).astype(jnp.bfloat16)
        every_value = jnp.concatenate([val_loc, summary_values], axis=0)
        out = jnp.einsum('kgts,skd->tkgd', weights.astype(jnp.float32), every_value.astype(jnp.float32))
        return out.reshape(TOK_DEV, HQ * HD).astype(jnp.bfloat16)
    attended = lax.map(attend, jnp.arange(shards, dtype=jnp.int32)).reshape(TOKENS, HQ * HD)
    hidden = jnp.dot(attended, out_weight, preferred_element_type=jnp.float32)
    normed = (normalize(hidden) * norm_gain.astype(jnp.float32)).astype(jnp.bfloat16)
    combine = route_scores / lax.optimization_barrier(jnp.sum(route_scores, axis=-1, keepdims=True))
    slots = shards * CAP

    def expert_step(total, expert):
        picked = routes == expert
        weight_tok = lax.optimization_barrier(jnp.sum(jnp.where(picked, combine, 0.0), axis=-1))
        chosen = jnp.any(picked, axis=-1)
        rows = jnp.nonzero(chosen, size=slots, fill_value=0)[0].astype(jnp.int32)
        used = jnp.arange(slots) < jnp.sum(chosen.astype(jnp.int32))
        inputs = normed[rows]
        gate = jnp.dot(inputs, expert_gate[expert], preferred_element_type=jnp.float32)
        upper = jnp.dot(inputs, expert_up[expert], preferred_element_type=jnp.float32)
        act = (jax.nn.silu(gate) * upper).astype(jnp.bfloat16)
        result = jnp.dot(act, expert_down[expert], preferred_element_type=jnp.float32).astype(jnp.bfloat16)
        contrib = jnp.where(used[:, None], weight_tok[rows][:, None] * result.astype(jnp.float32), 0.0)
        return (total.at[rows].add(contrib), None)
    total, _ = lax.scan(expert_step, jnp.zeros((TOKENS, D), jnp.float32), jnp.arange(EXPERTS, dtype=jnp.int32))
    return (hidden.astype(jnp.bfloat16), (hidden + total).astype(jnp.bfloat16))
```

```python
import functools
import math

import jax
import jax.numpy as jnp
from jax import lax
from jax.experimental import pallas as pl
from jax.experimental.pallas import tpu as pltpu
from jax.sharding import PartitionSpec as P

D = 2048
HQ = 16
KVH = 4
HD = 128
TOP = 8
EXP_DEV = 1
NB = 4


def normalize(x):
    return x * lax.rsqrt(jnp.mean(x * x, axis=-1, keepdims=True) + 1e-06)


RING_BYTES = 16 * 2**20
PASSES = 2


def chip_at(position, chips):
    depth = chips // 2
    y = position // depth
    return (position * (1 - y) + (chips - 1 - position) * y) * 2 + y


def layer_kernel(
    n,
    cap,
    queries,
    keys,
    values,
    blocks,
    weight_own,
    key_gain,
    norm_gain,
    routes,
    route_scores,
    gate_hbm,
    up_hbm,
    down_hbm,
    projected,
    out,
    normed,
    hidden,
    att,
    wq,
    outq,
    hidq,
    sums_own,
    sums,
    share,
    gate_w,
    up_w,
    down_w,
    tok,
    wbuf,
    rows_in,
    act,
    place,
    comb,
    mine,
    outgo,
    theirs,
    ring_in,
    load_sem,
    s_send,
    s_recv,
    wg_send,
    wg_recv,
    wp_send,
    wp_recv,
    at_send,
    at_recv,
    h_send,
    h_recv,
    w_send,
    w_recv,
    ag_send,
    ag_recv,
    pt_send,
    pt_recv,
    y_send,
    y_recv,
    rs_send_sem,
    rs_recv_sem,
):
    tokens = normed.shape[0]
    half = tokens // 2
    width = normed.shape[1]
    ff = gate_w.shape[1]
    chips = n // 2
    far = chips // 2
    me = lax.axis_index("ctx")
    core = me % 2
    y = (me // 2) % 2
    z = me // 4
    pos = z * (1 - y) + (chips - 1 - z) * y
    partner = me + 1 - 2 * core
    ahead = chip_at((pos + 1) % chips, chips) * 2 + core
    behind = chip_at((pos + chips - 1) % chips, chips) * 2 + core
    neighbour = (ahead, behind)

    loads = [
        pltpu.make_async_copy(a, b, load_sem.at[k])
        for k, (a, b) in enumerate(((gate_hbm, gate_w), (up_hbm, up_w), (down_hbm, down_w)))
    ]
    for load in loads:
        load.start()

    barrier = pltpu.get_barrier_semaphore()
    across = 1 - lax.axis_index("groups")

    def greet(k, _):
        pl.semaphore_signal(barrier, inc=1, device_id={"ctx": (me + k) % n})
        return 0

    lax.fori_loop(1, n, greet, 0)
    pl.semaphore_signal(barrier, inc=1, device_id={"groups": across})
    pl.semaphore_signal(barrier, inc=1, device_id={"groups": across, "ctx": partner})

    def mean_of(ref):
        shape = (2 * NB, tokens)
        ids = jnp.broadcast_to(blocks[...], shape)
        member = jnp.where(ids == lax.broadcasted_iota(jnp.int32, shape, 0) % NB, 1.0, 0.0)
        count = jnp.sum(member, axis=1, keepdims=True)
        return (
            jnp.dot(member.astype(jnp.bfloat16), ref[...], preferred_element_type=jnp.float32)
            / count
        )

    kmean, vmean = mean_of(keys), mean_of(values)
    upper = lax.broadcasted_iota(jnp.int32, (2 * NB, HD), 0) < NB
    for g in range(KVH):
        cols = slice(g * HD, (g + 1) * HD)
        sums_own[:, cols] = jnp.where(
            upper, normalize(kmean[:, cols]) * key_gain[...], normalize(vmean[:, cols])
        ).astype(jnp.bfloat16)
    pl.semaphore_wait(barrier, n + 1)

    def s_copy(k):
        target = (me + k) % n
        return pltpu.make_async_remote_copy(
            src_ref=sums_own,
            dst_ref=sums.at[me],
            send_sem=s_send.at[k],
            recv_sem=s_recv.at[k],
            device_id={"ctx": target},
        )

    def s_start(k, _):
        s_copy(k).start()
        return 0

    def s_wait(k, _):
        s_copy(k).wait()
        return 0

    lax.fori_loop(1, n, s_start, 0)
    sums[me] = sums_own[...]

    def rows(h):
        return pl.ds(h * half, half)

    def chip(offset):
        return (pos + offset + chips) % chips

    def ag_copy(d, step, h):
        sign = 1 - 2 * d
        q = chip(-sign * (step - 1))
        src = normed.at[rows(h)] if step == 1 else tok.at[q, core, rows(h)]
        return pltpu.make_async_remote_copy(
            src_ref=src,
            dst_ref=tok.at[q, core, rows(h)],
            send_sem=ag_send.at[d, step - 1, h],
            recv_sem=ag_recv.at[d, step - 1, h],
            device_id={"ctx": neighbour[d]},
        )

    def pt_copy(offset, h):
        q = chip(offset)
        src = normed.at[rows(h)] if offset == 0 else tok.at[q, core, rows(h)]
        return pltpu.make_async_remote_copy(
            src_ref=src,
            dst_ref=tok.at[q, core, rows(h)],
            send_sem=pt_send.at[offset % chips, h],
            recv_sem=pt_recv.at[offset % chips, h],
            device_id={"ctx": partner},
        )

    def order(d):
        return (0, 1) if d == 0 else (1, 0)

    wrows = weight_own.shape[0]
    passes, pcols = wq.shape[0], wq.shape[3]
    group = 1 - across
    slot = group * 2 + core

    def own_rows(t):
        return pl.ds(pl.multiple_of((core if t == 0 else 1 - core) * wrows, wrows), wrows)

    def w_cols(t, p):
        side = group * 2 + (core if t == 0 else 1 - core)
        return pl.ds(pl.multiple_of((side * passes + p) * pcols, pcols), pcols)

    def w_at(p, q, t):
        return wq.at[p, chip_at(q, chips), own_rows(t)]

    def wg_copy(d, step, p, t):
        sign = 1 - 2 * d
        if step == 1:
            src, dst = weight_own.at[:, w_cols(t, p)], w_at(p, pos, 0)
            target = neighbour[d] + t * (1 - 2 * core)
        else:
            src = dst = w_at(p, chip(-sign * (step - 1)), t)
            target = neighbour[d]
        return pltpu.make_async_remote_copy(
            src_ref=src,
            dst_ref=dst,
            send_sem=wg_send.at[d, step - 1, p, t],
            recv_sem=wg_recv.at[d, step - 1, p, t],
            device_id={"ctx": target},
        )

    def wp_copy(p):
        return pltpu.make_async_remote_copy(
            src_ref=weight_own.at[:, w_cols(1, p)],
            dst_ref=w_at(p, pos, 0),
            send_sem=wp_send.at[p],
            recv_sem=wp_recv.at[p],
            device_id={"ctx": partner},
        )

    def at_copy(kind, g):
        span = HQ // KVH * HD
        source = slot if kind < 2 else across * 2 + core
        block = att.at[
            pl.ds(pl.multiple_of(source * tokens, tokens), tokens), g * span : (g + 1) * span
        ]
        return pltpu.make_async_remote_copy(
            src_ref=block,
            dst_ref=block,
            send_sem=at_send.at[kind, g],
            recv_sem=at_recv.at[kind, g],
            device_id={"groups": across} if kind == 1 else {"ctx": partner},
        )

    def h_copy(kind, p):
        target = (
            {"ctx": partner},
            {"groups": across},
            {"groups": across, "ctx": partner},
        )[kind]
        theirs_slot = (group, across, across)[kind] * 2 + (1 - core, core, 1 - core)[kind]
        return pltpu.make_async_remote_copy(
            src_ref=outq.at[p, theirs_slot],
            dst_ref=hidq.at[slot, p],
            send_sem=h_send.at[kind, p],
            recv_sem=h_recv.at[kind, p],
            device_id=target,
        )

    for p in range(passes):
        for k in range(2):
            for d in range(2):
                wg_copy(d, 1, p, order(d)[k]).start()
    for p in range(passes):
        wp_copy(p).start()
        wq[p, chip_at(pos, chips), own_rows(0)] = weight_own[:, w_cols(0, p)]

    def w_copy(k):
        target = (me + k) % n
        return pltpu.make_async_remote_copy(
            src_ref=share.at[target],
            dst_ref=wbuf.at[pos * 2 + core],
            send_sem=w_send.at[k],
            recv_sem=w_recv.at[k],
            device_id={"ctx": target},
        )

    def w_start(k, _):
        w_copy(k).start()
        return 0

    def w_wait(k, _):
        w_copy(k).wait()
        return 0

    chosen_scores = route_scores[...]
    combine = chosen_scores / jnp.sum(chosen_scores, axis=0, keepdims=True)
    expert = lax.broadcasted_iota(jnp.int32, (n, tokens), 0)
    table_of = jnp.zeros((n, tokens), jnp.float32)
    for c in range(TOP):
        table_of = table_of + jnp.where(routes[c : c + 1] == expert, combine[c : c + 1], 0.0)
    for e in range(n):
        share[e] = jnp.broadcast_to(table_of[e : e + 1], (8, tokens))
    lax.fori_loop(1, n, w_start, 0)
    wbuf[pos * 2 + core] = share[me]
    lax.fori_loop(1, n, s_wait, 0)

    many = HQ // KVH
    scale = 1.0 / math.sqrt(HD)
    tall = (many * tokens, tokens)
    causal = lax.broadcasted_iota(jnp.int32, tall, 0) % tokens >= lax.broadcasted_iota(
        jnp.int32, tall, 1
    )
    far_shape = (many * tokens, n * 2 * NB)
    entry = lax.broadcasted_iota(jnp.int32, far_shape, 1)
    seen = (entry % (2 * NB) < NB) & (entry // (2 * NB) < me)
    contract_last = (((1,), (1,)), ((), ()))

    def attend(g):
        cols = slice(g * HD, (g + 1) * HD)
        heads = [slice((g * many + i) * HD, (g * many + i + 1) * HD) for i in range(many)]
        q = jnp.concatenate([queries[:, c] for c in heads], axis=0)
        table = sums[:, :, cols].astype(jnp.float32).reshape(n * 2 * NB, HD)
        shifted = jnp.concatenate([table[NB:], table[:NB]], axis=0).astype(jnp.bfloat16)
        table = table.astype(jnp.bfloat16)
        near = (
            lax.dot_general(q, keys[:, cols], contract_last, preferred_element_type=jnp.float32)
            * scale
        )
        near = jnp.where(causal, near, -jnp.inf)
        remote = lax.dot_general(q, table, contract_last, preferred_element_type=jnp.float32) * scale
        remote = jnp.where(seen, remote, -jnp.inf)
        top = jnp.maximum(
            jnp.max(near, axis=1, keepdims=True), jnp.max(remote, axis=1, keepdims=True)
        )
        near, remote = jnp.exp(near - top), jnp.exp(remote - top)
        total = jnp.sum(near, axis=1, keepdims=True) + jnp.sum(remote, axis=1, keepdims=True)
        near, remote = (near / total).astype(jnp.bfloat16), (remote / total).astype(jnp.bfloat16)
        result = jnp.dot(
            near, values[:, cols], preferred_element_type=jnp.float32
        ) + jnp.dot(remote, shifted, preferred_element_type=jnp.float32)
        result = result.astype(jnp.bfloat16)
        for i, c in enumerate(heads):
            att[pl.ds(pl.multiple_of(slot * tokens, tokens), tokens), c] = result[
                i * tokens : (i + 1) * tokens
            ]
        at_copy(1, g).start()
        at_copy(0, g).start()

    def project(p):
        weight = wq[p].reshape(chips * 2 * wrows, pcols)
        for side in (across, group):
            left = att[pl.ds(pl.multiple_of(side * 2 * tokens, 2 * tokens), 2 * tokens)]
            part = jnp.dot(left, weight, preferred_element_type=jnp.float32).astype(jnp.bfloat16)
            for c in range(2):
                outq[p, side * 2 + c] = part[c * tokens : (c + 1) * tokens]
            if side is across:
                h_copy(1, p).start()
                h_copy(2, p).start()
            else:
                h_copy(0, p).start()
        hidq[slot, p] = outq[p, slot]

    def w_step(step, p):
        for k in range(2):
            for d in range(2):
                t = order(d)[k]
                if step < far or k == 0:
                    wg_copy(d, step, p, t).wait_recv()
                if step + 1 < far or (step + 1 == far and k == 0):
                    wg_copy(d, step + 1, p, t).start()

    for g in range(KVH):
        attend(g)
        if g > 0:
            at_copy(1, g - 1).wait_recv()
            at_copy(2, g - 1).start()
        if g + 1 < far:
            for p in range(passes):
                w_step(g + 1, p)
    at_copy(1, KVH - 1).wait_recv()
    at_copy(2, KVH - 1).start()
    for p in range(passes):
        wp_copy(p).wait_recv()
    for g in range(KVH):
        at_copy(0, g).wait_recv()
        at_copy(2, g).wait_recv()
    for p in range(passes):
        for step in range(min(KVH + 1, far), far + 1):
            w_step(step, p)
        project(p)
    for p in range(passes):
        for kind in range(3):
            h_copy(kind, p).wait_recv()
        for s in range(4):
            at = (s * passes + p) * pcols
            hidden[:, at : at + pcols] = hidq[s, p].astype(jnp.float32)
    for h in range(2):
        hid = hidden[rows(h)]
        projected[rows(h)] = hid.astype(jnp.bfloat16)
        tidy = (normalize(hid) * norm_gain[...]).astype(jnp.bfloat16)
        normed[rows(h)] = tidy
        tok[pos, core, rows(h)] = tidy

    for k in range(2):
        for d in range(2):
            ag_copy(d, 1, order(d)[k]).start()
    for h in range(2):
        pt_copy(0, h).start()

    lax.fori_loop(1, n, w_wait, 0)
    for load in loads:
        load.wait()

    def y_copy(offset):
        q = chip(offset)
        return pltpu.make_async_remote_copy(
            src_ref=outgo.at[q],
            dst_ref=theirs.at[q],
            send_sem=y_send.at[offset % chips],
            recv_sem=y_recv.at[offset % chips],
            device_id={"ctx": partner},
        )

    def compute(offset):
        q = chip(offset)
        for h in range(2):
            pt_copy(offset, h).wait_recv()
        earlier = lax.broadcasted_iota(jnp.int32, (tokens, tokens), 0) < lax.broadcasted_iota(
            jnp.int32, (tokens, tokens), 1
        )
        earlier = jnp.where(earlier, 1.0, 0.0).astype(jnp.bfloat16)
        line = lax.broadcasted_iota(jnp.int32, (cap, tokens), 0).astype(jnp.float32)
        for rel in range(2):
            side = (core + rel) % 2
            weight = wbuf[q * 2 + side]
            chosen = jnp.where(weight > 0.0, 1.0, 0.0)
            slot = jnp.dot(chosen.astype(jnp.bfloat16), earlier, preferred_element_type=jnp.float32)
            slot = jnp.where(weight > 0.0, slot, -1.0)
            hit = jnp.broadcast_to(slot[0:1], (cap, tokens)) == line
            pick = jnp.where(hit, 1.0, 0.0).astype(jnp.bfloat16)
            place[rel] = pick
            scaled = jnp.where(hit, jnp.broadcast_to(weight[0:1], (cap, tokens)), 0.0)
            comb[rel] = jnp.broadcast_to(jnp.sum(scaled, axis=1, keepdims=True), (cap, 128))
            for c in range(0, width, 512):
                rows_in[rel * cap : (rel + 1) * cap, c : c + 512] = jnp.dot(
                    pick, tok[q, side, :, c : c + 512], preferred_element_type=jnp.float32
                ).astype(jnp.bfloat16)

        def in_tile(k, _):
            cols = pl.ds(pl.multiple_of(k * 256, 256), 256)
            x = rows_in[...]
            g = jnp.dot(x, gate_w[:, cols], preferred_element_type=jnp.float32)
            u = jnp.dot(x, up_w[:, cols], preferred_element_type=jnp.float32)
            act[:, cols] = (g / (1.0 + jnp.exp(-g)) * u).astype(jnp.bfloat16)
            return 0

        lax.fori_loop(0, ff // 256, in_tile, 0)

        def out_tile(k, _):
            cols = pl.ds(pl.multiple_of(k * 512, 512), 512)
            r = jnp.dot(act[...], down_w[:, cols], preferred_element_type=jnp.float32)
            r = r.astype(jnp.bfloat16).astype(jnp.float32)
            for rel, dest in ((0, mine), (1, outgo)):
                part = r[rel * cap : (rel + 1) * cap] * comb[rel][:, 0:1]
                dest[q, :, cols] = lax.dot_general(
                    place[rel],
                    part.astype(jnp.bfloat16),
                    (((0,), (0,)), ((), ())),
                    preferred_element_type=jnp.float32,
                ).astype(jnp.bfloat16)
            return 0

        lax.fori_loop(0, width // 512, out_tile, 0)
        y_copy(offset).start()

    for step in range(1, far):
        for k in range(2):
            for d in range(2):
                h = order(d)[k]
                sign = 1 - 2 * d
                ag_copy(d, step, h).wait_recv()
                if step + 1 < far or k == 0:
                    ag_copy(d, step + 1, h).start()
                pt_copy(-sign * step, h).start()
            if step == 1:
                if k == 0:
                    compute(0)
            else:
                compute((step - 1) * (2 * k - 1))
    compute(1 - far)
    compute(far - 1)
    for d in range(2):
        h = order(d)[0]
        ag_copy(d, far, h).wait_recv()
        pt_copy(far, h).start()

    def sum_of(q, h):
        return mine[q, rows(h)].astype(jnp.float32) + theirs[q, rows(h)].astype(jnp.float32)

    def rs_copy(d, step, h, src):
        return pltpu.make_async_remote_copy(
            src_ref=src,
            dst_ref=ring_in.at[d, step - 1, h],
            send_sem=rs_send_sem.at[d, step - 1, h],
            recv_sem=rs_recv_sem.at[d, step - 1, h],
            device_id={"ctx": neighbour[d]},
        )

    def rs_step(d, step, k):
        h = order(d)[k]
        sign = 1 - 2 * d
        q = chip(sign * (far + 1 - step))
        if step == 1 or (step == 2 and k == 1):
            mine[q, rows(h)] = sum_of(q, h).astype(jnp.bfloat16)
            src = mine.at[q, rows(h)]
        else:
            src = ring_in.at[d, step - 2, h]
            rs_copy(d, step - 1, h, src).wait_recv()
            ring_in[d, step - 2, h] = (
                ring_in[d, step - 2, h].astype(jnp.float32) + sum_of(q, h)
            ).astype(jnp.bfloat16)
        rs_copy(d, step, h, src).start()

    for offset in range(chips):
        if offset != far:
            y_copy(offset).wait_recv()
    for d in range(2):
        rs_step(d, 2, 1)
    compute(far)
    y_copy(far).wait_recv()
    sends = [(1, 0)]
    for step in range(2, far + 1):
        if step < far:
            sends += [(step + 1, 1)]
        sends += [(step, 0)]
    for step, k in sends:
        for d in range(2):
            rs_step(d, step, k)
    for h in range(2):
        total = hidden[rows(h)] + sum_of(pos, h)
        for d in range(2):
            rs_copy(d, far, h, ring_in.at[d, far - 1, h]).wait_recv()
            total = total + ring_in[d, far - 1, h].astype(jnp.float32)
        out[rows(h)] = total.astype(jnp.bfloat16)

    for d in range(2):
        for step in range(1, far + 1):
            for k in range(2):
                h = order(d)[k]
                if step < far or k == 0:
                    ag_copy(d, step, h).wait_send()
                if step > 1 or k == 0:
                    rs_copy(d, step, h, ring_in.at[d, step - 1, h]).wait_send()
    for offset in range(chips):
        for h in range(2):
            pt_copy(offset, h).wait_send()
        y_copy(offset).wait_send()


    for p in range(passes):
        for d in range(2):
            for step in range(1, far + 1):
                for k in range(2):
                    if step < far or k == 0:
                        wg_copy(d, step, p, order(d)[k]).wait_send()
        wp_copy(p).wait_send()
        for kind in range(3):
            h_copy(kind, p).wait_send()
    for g in range(KVH):
        for kind in range(3):
            at_copy(kind, g).wait_send()


def write_kernel(a, b, a_out, b_out, sem):
    copies = [
        pltpu.make_async_copy(x, y, sem.at[k]) for k, (x, y) in enumerate(((a, a_out), (b, b_out)))
    ]
    for copy in copies:
        copy.start()
    for copy in copies:
        copy.wait()


def layer_ring(
    queries,
    keys,
    values,
    block_ids,
    out_weight,
    summary_gain,
    norm_gain,
    routes,
    route_scores,
    expert_gate,
    expert_up,
    expert_down,
    n,
    cap,
):
    tokens, width = queries.shape
    ff = expert_gate.shape[-1]
    chips = n // 2
    far = chips // 2
    vmem = pl.BlockSpec(memory_space=pltpu.VMEM)
    hbm = pl.BlockSpec(memory_space=pl.ANY)
    dma = pltpu.SemaphoreType.DMA
    bf16, f32 = jnp.bfloat16, jnp.float32
    result = jax.ShapeDtypeStruct((tokens, width), bf16)
    pair = pl.pallas_call(
        functools.partial(layer_kernel, n, cap),
        out_shape=(result, result),
        in_specs=[vmem] * 9 + [hbm] * 3,
        out_specs=(vmem, vmem),
        scratch_shapes=[
            pltpu.VMEM((tokens, width), bf16),
            pltpu.VMEM((tokens, width), f32),
            pltpu.VMEM((4 * tokens, width), bf16),
            pltpu.VMEM((PASSES, chips, 2 * out_weight.shape[0], width // (4 * PASSES)), bf16),
            pltpu.VMEM((PASSES, 4, tokens, width // (4 * PASSES)), bf16),
            pltpu.VMEM((4, PASSES, tokens, width // (4 * PASSES)), bf16),
            pltpu.VMEM((2 * NB, KVH * HD), bf16),
            pltpu.VMEM((n, 2 * NB, KVH * HD), bf16),
            pltpu.VMEM((n, 8, tokens), f32),
            pltpu.VMEM((width, ff), bf16),
            pltpu.VMEM((width, ff), bf16),
            pltpu.VMEM((ff, width), bf16),
            pltpu.VMEM((chips, 2, tokens, width), bf16),
            pltpu.VMEM((n, 8, tokens), f32),
            pltpu.VMEM((2 * cap, width), bf16),
            pltpu.VMEM((2 * cap, ff), bf16),
            pltpu.VMEM((2, cap, tokens), bf16),
            pltpu.VMEM((2, cap, 128), f32),
            pltpu.VMEM((chips, tokens, width), bf16),
            pltpu.VMEM((chips, tokens, width), bf16),
            pltpu.VMEM((chips, tokens, width), bf16),
            pltpu.VMEM((2, far, 2, tokens // 2, width), bf16),
            dma((3,)),
            dma((n,)),
            dma((n,)),
            dma((2, far, PASSES, 2)),
            dma((2, far, PASSES, 2)),
            dma((PASSES,)),
            dma((PASSES,)),
            dma((3, KVH)),
            dma((3, KVH)),
            dma((3, PASSES)),
            dma((3, PASSES)),
            dma((n,)),
            dma((n,)),
            dma((2, far, 2)),
            dma((2, far, 2)),
            dma((chips, 2)),
            dma((chips, 2)),
            dma((chips,)),
            dma((chips,)),
            dma((2, far, 2)),
            dma((2, far, 2)),
        ],
        compiler_params=pltpu.CompilerParams(
            collective_id=1, has_side_effects=True, vmem_limit_bytes=62 * 2**20
        ),
    )(
        queries,
        keys,
        values,
        block_ids[None, :],
        out_weight,
        summary_gain[None, :],
        norm_gain[None, :],
        routes.T,
        route_scores.T,
        expert_gate[0],
        expert_up[0],
        expert_down[0],
    )
    return pl.pallas_call(
        write_kernel,
        out_shape=(result, result),
        in_specs=[vmem] * 2,
        out_specs=(hbm, hbm),
        scratch_shapes=[dma((2,))],
    )(*pair)


def body(
    queries,
    keys,
    values,
    block_ids,
    out_weight,
    summary_gain,
    norm_gain,
    routes,
    route_scores,
    expert_gate,
    expert_up,
    expert_down,
):
    tokens_here = queries.shape[0]
    combine = route_scores / jnp.sum(route_scores, axis=-1, keepdims=True)
    experts_all = EXP_DEV * lax.axis_size("ctx")
    capacity = max(2, 5 * tokens_here * TOP // (4 * experts_all))
    chips = experts_all // 2
    fits = experts_all * tokens_here * D * 2 <= RING_BYTES
    if fits and chips % 4 == 0 and lax.axis_size("groups") == 2:
        return layer_ring(
            queries,
            keys,
            values,
            block_ids,
            out_weight,
            summary_gain,
            norm_gain,
            routes,
            route_scores,
            expert_gate,
            expert_up,
            expert_down,
            experts_all,
            -(-capacity // 16) * 16,
        )
    group = HQ // KVH
    scale = 1.0 / math.sqrt(HD)
    member = block_ids[None, :] == jnp.arange(NB, dtype=jnp.int32)[:, None]
    count = jnp.sum(member.astype(jnp.float32), axis=-1)
    indicator = member.astype(jnp.bfloat16)
    kmean = jnp.dot(indicator, keys, preferred_element_type=jnp.float32) / count[:, None]
    vmean = jnp.dot(indicator, values, preferred_element_type=jnp.float32) / count[:, None]
    summary_keys = (
        (normalize(kmean.reshape(NB, KVH, HD)) * summary_gain)
        .astype(jnp.bfloat16)
        .reshape(NB, KVH * HD)
    )
    summary_values = (
        normalize(vmean.reshape(NB, KVH, HD)).astype(jnp.bfloat16).reshape(NB, KVH * HD)
    )
    summaries = lax.all_gather(
        jnp.concatenate([summary_keys, summary_values], axis=1), "ctx", axis=0, tiled=True
    )
    all_keys, all_values = summaries[:, : KVH * HD], summaries[:, KVH * HD :]
    index = lax.axis_index("ctx")
    query = queries.reshape(tokens_here, KVH, group, HD)
    key_loc = keys.reshape(tokens_here, KVH, HD)
    remote_keys = all_keys.reshape(-1, KVH, HD)
    causal = jnp.arange(tokens_here)[:, None] >= jnp.arange(tokens_here)[None, :]
    owner = jnp.arange(remote_keys.shape[0], dtype=jnp.int32) // NB
    local = jnp.einsum("tkgd,skd->kgts", query, key_loc, preferred_element_type=jnp.float32) * scale
    local = jnp.where(causal[None, None], local, -jnp.inf)
    remote = (
        jnp.einsum("tkgd,skd->kgts", query, remote_keys, preferred_element_type=jnp.float32) * scale
    )
    remote = jnp.where((owner < index)[None, None, None, :], remote, -jnp.inf)
    scores = jnp.concatenate([local, remote], axis=-1)
    top = jnp.max(scores, axis=-1, keepdims=True)
    expo = jnp.exp(scores - top)
    weights = (expo / jnp.sum(expo, axis=-1, keepdims=True)).astype(jnp.bfloat16)
    every_value = jnp.concatenate(
        [values.reshape(tokens_here, KVH, HD), all_values.reshape(-1, KVH, HD)], axis=0
    )
    attended = jnp.einsum(
        "kgts,skd->tkgd", weights, every_value, preferred_element_type=jnp.float32
    )
    attended = attended.reshape(tokens_here, HQ * HD).astype(jnp.bfloat16)
    hidden = jnp.dot(
        attended,
        lax.all_gather(out_weight, "ctx", axis=0, tiled=True),
        preferred_element_type=jnp.float32,
    )
    normed = (normalize(hidden) * norm_gain).astype(jnp.bfloat16)
    flat_routes = routes.reshape(-1)
    hits = (flat_routes[:, None] == jnp.arange(experts_all, dtype=jnp.int32)[None, :]).astype(
        jnp.int32
    )
    slot = jnp.sum(hits * (jnp.cumsum(hits, axis=0) - 1), axis=-1)
    target = flat_routes * capacity + slot
    source = jnp.arange(tokens_here * TOP, dtype=jnp.int32) // TOP
    outgoing = jnp.zeros((experts_all * capacity, D), jnp.bfloat16).at[target].set(normed[source])
    outgoing = outgoing.reshape(experts_all, capacity, D)
    arrived = lax.all_to_all(outgoing, "ctx", split_axis=0, concat_axis=0, tiled=True)
    senders = arrived.shape[0] // EXP_DEV
    width = arrived.shape[1]
    inputs = (
        arrived.reshape(senders, EXP_DEV, width, D)
        .transpose(1, 0, 2, 3)
        .reshape(EXP_DEV, senders * width, D)
    )
    gate = jnp.einsum("erd,edf->erf", inputs, expert_gate, preferred_element_type=jnp.float32)
    upper = jnp.einsum("erd,edf->erf", inputs, expert_up, preferred_element_type=jnp.float32)
    act = (jax.nn.silu(gate) * upper).astype(jnp.bfloat16)
    result = jnp.einsum(
        "erf,efd->erd", act, expert_down, preferred_element_type=jnp.float32
    ).astype(jnp.bfloat16)
    result = (
        result.reshape(EXP_DEV, senders, width, D)
        .transpose(1, 0, 2, 3)
        .reshape(senders * EXP_DEV, width, D)
    )
    returned = lax.all_to_all(result, "ctx", split_axis=0, concat_axis=0, tiled=True)
    returned = returned.reshape(experts_all * capacity, D)
    picked = jnp.take(returned, target, axis=0).reshape(tokens_here, TOP, D)
    blended = jnp.sum(combine[:, :, None] * picked.astype(jnp.float32), axis=1)
    return (hidden.astype(jnp.bfloat16), (hidden + blended).astype(jnp.bfloat16))


def solution(mesh):
    in_specs = (
        P(("groups", "ctx"), None),
        P(("groups", "ctx"), None),
        P(("groups", "ctx"), None),
        P(("groups", "ctx")),
        P("ctx", None),
        P(),
        P(),
        P(("groups", "ctx"), None),
        P(("groups", "ctx"), None),
        P("ctx", None, None),
        P("ctx", None, None),
        P("ctx", None, None),
    )
    out_specs = (P(("groups", "ctx"), None), P(("groups", "ctx"), None))
    return jax.shard_map(body, mesh=mesh, in_specs=in_specs, out_specs=out_specs, check_vma=False)
```

```python
import functools
import math

import jax
import jax.numpy as jnp
from jax import lax
from jax.experimental import pallas as pl
from jax.experimental.pallas import tpu as pltpu
from jax.sharding import PartitionSpec as P

D = 2048
HQ = 16
KVH = 4
HD = 128
TOP = 8
EXP_DEV = 1
NB = 4


def normalize(x):
    return x * lax.rsqrt(jnp.mean(x * x, axis=-1, keepdims=True) + 1e-06)


RING_BYTES = 16 * 2**20
PASSES = 2
OUT_TILE = 1024


def chip_at(position, chips):
    depth = chips // 2
    y = position // depth
    return (position * (1 - y) + (chips - 1 - position) * y) * 2 + y


def layer_kernel(
    n,
    cap,
    queries,
    keys,
    values,
    blocks,
    weight_own,
    key_gain,
    norm_gain,
    routes,
    route_scores,
    gate_hbm,
    up_hbm,
    down_hbm,
    projected,
    out,
    normed,
    hidden,
    att,
    wq,
    outq,
    hidq,
    sums_own,
    sums,
    share,
    gate_w,
    up_w,
    down_w,
    tok,
    wbuf,
    slots,
    rows_in,
    act,
    place,
    comb,
    mine,
    outgo,
    theirs,
    ring_in,
    load_sem,
    s_send,
    s_recv,
    wg_send,
    wg_recv,
    wp_send,
    wp_recv,
    at_send,
    at_recv,
    h_send,
    h_recv,
    w_send,
    w_recv,
    ag_send,
    ag_recv,
    pt_send,
    pt_recv,
    y_send,
    y_recv,
    rs_send_sem,
    rs_recv_sem,
):
    tokens = normed.shape[0]
    half = tokens // 2
    width = normed.shape[1]
    ff = gate_w.shape[1]
    chips = n // 2
    far = chips // 2
    me = lax.axis_index("ctx")
    core = me % 2
    y = (me // 2) % 2
    z = me // 4
    pos = z * (1 - y) + (chips - 1 - z) * y
    partner = me + 1 - 2 * core
    ahead = chip_at((pos + 1) % chips, chips) * 2 + core
    behind = chip_at((pos + chips - 1) % chips, chips) * 2 + core
    neighbour = (ahead, behind)

    loads = [
        pltpu.make_async_copy(a, b, load_sem.at[k])
        for k, (a, b) in enumerate(((gate_hbm, gate_w), (up_hbm, up_w), (down_hbm, down_w)))
    ]
    for load in loads:
        load.start()

    barrier = pltpu.get_barrier_semaphore()
    across = 1 - lax.axis_index("groups")

    def greet(k, _):
        pl.semaphore_signal(barrier, inc=1, device_id={"ctx": (me + k) % n})
        return 0

    lax.fori_loop(1, n, greet, 0)
    pl.semaphore_signal(barrier, inc=1, device_id={"groups": across})
    pl.semaphore_signal(barrier, inc=1, device_id={"groups": across, "ctx": partner})

    def mean_of(ref):
        shape = (2 * NB, tokens)
        ids = jnp.broadcast_to(blocks[...], shape)
        member = jnp.where(ids == lax.broadcasted_iota(jnp.int32, shape, 0) % NB, 1.0, 0.0)
        count = jnp.sum(member, axis=1, keepdims=True)
        return (
            jnp.dot(member.astype(jnp.bfloat16), ref[...], preferred_element_type=jnp.float32)
            / count
        )

    kmean, vmean = mean_of(keys), mean_of(values)
    upper = lax.broadcasted_iota(jnp.int32, (2 * NB, HD), 0) < NB
    for g in range(KVH):
        cols = slice(g * HD, (g + 1) * HD)
        sums_own[:, cols] = jnp.where(
            upper, normalize(kmean[:, cols]) * key_gain[...], normalize(vmean[:, cols])
        ).astype(jnp.bfloat16)
    pl.semaphore_wait(barrier, n + 1)

    def s_copy(k):
        return pltpu.make_async_remote_copy(
            src_ref=sums_own,
            dst_ref=sums.at[me],
            send_sem=s_send.at[k],
            recv_sem=s_recv.at[k],
            device_id={"ctx": (me + 2 * k) % n},
        )

    def sp_copy(k):
        source = (me + n - 2 * k) % n
        return pltpu.make_async_remote_copy(
            src_ref=sums.at[source],
            dst_ref=sums.at[source],
            send_sem=s_send.at[chips + k],
            recv_sem=s_recv.at[chips + k],
            device_id={"ctx": partner},
        )

    own_copy = pltpu.make_async_remote_copy(
        src_ref=sums_own,
        dst_ref=sums.at[me],
        send_sem=s_send.at[chips],
        recv_sem=s_recv.at[chips],
        device_id={"ctx": partner},
    )

    def s_start(k, _):
        s_copy(k).start()
        return 0

    def s_pass(k, _):
        s_copy(k).wait_recv()
        sp_copy(k).start()
        return 0

    def s_wait(k, _):
        sp_copy(k).wait_recv()
        s_copy(k).wait_send()
        sp_copy(k).wait_send()
        return 0

    lax.fori_loop(1, chips, s_start, 0)
    own_copy.start()
    sums[me] = sums_own[...]

    def rows(h):
        return pl.ds(h * half, half)

    def chip(offset):
        return (pos + offset + chips) % chips

    def ag_copy(d, step, h):
        sign = 1 - 2 * d
        q = chip(-sign * (step - 1))
        src = normed.at[rows(h)] if step == 1 else tok.at[q, core, rows(h)]
        return pltpu.make_async_remote_copy(
            src_ref=src,
            dst_ref=tok.at[q, core, rows(h)],
            send_sem=ag_send.at[d, step - 1, h],
            recv_sem=ag_recv.at[d, step - 1, h],
            device_id={"ctx": neighbour[d]},
        )

    def pt_copy(offset, h):
        q = chip(offset)
        src = normed.at[rows(h)] if offset == 0 else tok.at[q, core, rows(h)]
        return pltpu.make_async_remote_copy(
            src_ref=src,
            dst_ref=tok.at[q, core, rows(h)],
            send_sem=pt_send.at[offset % chips, h],
            recv_sem=pt_recv.at[offset % chips, h],
            device_id={"ctx": partner},
        )

    def order(d):
        return (0, 1) if d == 0 else (1, 0)

    wrows = weight_own.shape[0]
    passes, pcols = wq.shape[0], wq.shape[3]
    group = 1 - across
    slot = group * 2 + core

    def own_rows(t):
        return pl.ds(pl.multiple_of((core if t == 0 else 1 - core) * wrows, wrows), wrows)

    def w_cols(t, p):
        side = group * 2 + (core if t == 0 else 1 - core)
        return pl.ds(pl.multiple_of((side * passes + p) * pcols, pcols), pcols)

    def w_at(p, q, t):
        return wq.at[p, chip_at(q, chips), own_rows(t)]

    def wg_copy(d, step, p, t):
        sign = 1 - 2 * d
        if step == 1:
            src, dst = weight_own.at[:, w_cols(t, p)], w_at(p, pos, 0)
            target = neighbour[d] + t * (1 - 2 * core)
        else:
            src = dst = w_at(p, chip(-sign * (step - 1)), t)
            target = neighbour[d]
        return pltpu.make_async_remote_copy(
            src_ref=src,
            dst_ref=dst,
            send_sem=wg_send.at[d, step - 1, p, t],
            recv_sem=wg_recv.at[d, step - 1, p, t],
            device_id={"ctx": target},
        )

    def wp_copy(p):
        return pltpu.make_async_remote_copy(
            src_ref=weight_own.at[:, w_cols(1, p)],
            dst_ref=w_at(p, pos, 0),
            send_sem=wp_send.at[p],
            recv_sem=wp_recv.at[p],
            device_id={"ctx": partner},
        )

    def at_copy(kind, g):
        span = HQ // KVH * HD
        source = slot if kind < 2 else across * 2 + core
        block = att.at[
            pl.ds(pl.multiple_of(source * tokens, tokens), tokens), g * span : (g + 1) * span
        ]
        return pltpu.make_async_remote_copy(
            src_ref=block,
            dst_ref=block,
            send_sem=at_send.at[kind, g],
            recv_sem=at_recv.at[kind, g],
            device_id={"groups": across} if kind == 1 else {"ctx": partner},
        )

    def h_copy(kind, p):
        target = (
            {"ctx": partner},
            {"groups": across},
            {"groups": across, "ctx": partner},
        )[kind]
        theirs_slot = (group, across, across)[kind] * 2 + (1 - core, core, 1 - core)[kind]
        return pltpu.make_async_remote_copy(
            src_ref=outq.at[p, theirs_slot],
            dst_ref=hidq.at[slot, p],
            send_sem=h_send.at[kind, p],
            recv_sem=h_recv.at[kind, p],
            device_id=target,
        )

    for p in range(passes):
        for k in range(2):
            for d in range(2):
                wg_copy(d, 1, p, order(d)[k]).start()
    for p in range(passes):
        wp_copy(p).start()
        wq[p, chip_at(pos, chips), own_rows(0)] = weight_own[:, w_cols(0, p)]

    def w_copy(k):
        target = (me + k) % n
        return pltpu.make_async_remote_copy(
            src_ref=share.at[target],
            dst_ref=wbuf.at[pos * 2 + core],
            send_sem=w_send.at[k],
            recv_sem=w_recv.at[k],
            device_id={"ctx": target},
        )

    def w_start(k, _):
        w_copy(k).start()
        return 0

    def w_wait(k, _):
        w_copy(k).wait()
        return 0

    chosen_scores = route_scores[...]
    combine = chosen_scores / jnp.sum(chosen_scores, axis=0, keepdims=True)
    expert = lax.broadcasted_iota(jnp.int32, (n, tokens), 0)
    table_of = jnp.zeros((n, tokens), jnp.float32)
    for c in range(TOP):
        table_of = table_of + jnp.where(routes[c : c + 1] == expert, combine[c : c + 1], 0.0)
    for e in range(n):
        share[e] = table_of[e : e + 1]
    lax.fori_loop(1, n, w_start, 0)
    wbuf[pos * 2 + core] = share[me]
    lax.fori_loop(1, chips, s_pass, 0)
    own_copy.wait()
    lax.fori_loop(1, chips, s_wait, 0)

    many = HQ // KVH
    scale = 1.0 / math.sqrt(HD)
    tall = (many * tokens, tokens)
    causal = lax.broadcasted_iota(jnp.int32, tall, 0) % tokens >= lax.broadcasted_iota(
        jnp.int32, tall, 1
    )
    far_shape = (many * tokens, n * 2 * NB)
    entry = lax.broadcasted_iota(jnp.int32, far_shape, 1)
    seen = (entry % (2 * NB) < NB) & (entry // (2 * NB) < me)
    contract_last = (((1,), (1,)), ((), ()))

    def attend(g):
        cols = slice(g * HD, (g + 1) * HD)
        heads = [slice((g * many + i) * HD, (g * many + i + 1) * HD) for i in range(many)]
        q = jnp.concatenate([queries[:, c] for c in heads], axis=0)
        table = sums[:, :, cols].astype(jnp.float32).reshape(n * 2 * NB, HD)
        shifted = jnp.concatenate([table[NB:], table[:NB]], axis=0).astype(jnp.bfloat16)
        table = table.astype(jnp.bfloat16)
        near = (
            lax.dot_general(q, keys[:, cols], contract_last, preferred_element_type=jnp.float32)
            * scale
        )
        near = jnp.where(causal, near, -jnp.inf)
        remote = lax.dot_general(q, table, contract_last, preferred_element_type=jnp.float32) * scale
        remote = jnp.where(seen, remote, -jnp.inf)
        top = jnp.maximum(
            jnp.max(near, axis=1, keepdims=True), jnp.max(remote, axis=1, keepdims=True)
        )
        near, remote = jnp.exp(near - top), jnp.exp(remote - top)
        total = jnp.sum(near, axis=1, keepdims=True) + jnp.sum(remote, axis=1, keepdims=True)
        near, remote = (near / total).astype(jnp.bfloat16), (remote / total).astype(jnp.bfloat16)
        result = jnp.dot(
            near, values[:, cols], preferred_element_type=jnp.float32
        ) + jnp.dot(remote, shifted, preferred_element_type=jnp.float32)
        result = result.astype(jnp.bfloat16)
        for i, c in enumerate(heads):
            att[pl.ds(pl.multiple_of(slot * tokens, tokens), tokens), c] = result[
                i * tokens : (i + 1) * tokens
            ]
        at_copy(1, g).start()
        at_copy(0, g).start()

    def project(p):
        weight = wq[p].reshape(chips * 2 * wrows, pcols)
        for side in (across, group):
            left = att[pl.ds(pl.multiple_of(side * 2 * tokens, 2 * tokens), 2 * tokens)]
            part = jnp.dot(left, weight, preferred_element_type=jnp.float32).astype(jnp.bfloat16)
            for c in range(2):
                outq[p, side * 2 + c] = part[c * tokens : (c + 1) * tokens]
            if side is across:
                h_copy(1, p).start()
                h_copy(2, p).start()
            else:
                h_copy(0, p).start()
        hidq[slot, p] = outq[p, slot]

    def w_step(step, p):
        for k in range(2):
            for d in range(2):
                t = order(d)[k]
                if step < far or k == 0:
                    wg_copy(d, step, p, t).wait_recv()
                if step + 1 < far or (step + 1 == far and k == 0):
                    wg_copy(d, step + 1, p, t).start()

    for g in range(KVH):
        attend(g)
        if g > 0:
            at_copy(1, g - 1).wait_recv()
            at_copy(2, g - 1).start()
        if g + 1 < far:
            for p in range(passes):
                w_step(g + 1, p)
    at_copy(1, KVH - 1).wait_recv()
    at_copy(2, KVH - 1).start()
    for p in range(passes):
        wp_copy(p).wait_recv()
    for g in range(KVH):
        at_copy(0, g).wait_recv()
        at_copy(2, g).wait_recv()
    for p in range(passes):
        for step in range(min(KVH + 1, far), far + 1):
            w_step(step, p)
        project(p)
    for p in range(passes):
        for kind in range(3):
            h_copy(kind, p).wait_recv()
        for s in range(4):
            at = (s * passes + p) * pcols
            hidden[:, at : at + pcols] = hidq[s, p].astype(jnp.float32)
    for h in range(2):
        hid = hidden[rows(h)]
        projected[rows(h)] = hid.astype(jnp.bfloat16)
        tidy = (normalize(hid) * norm_gain[...]).astype(jnp.bfloat16)
        normed[rows(h)] = tidy
        tok[pos, core, rows(h)] = tidy

    for k in range(2):
        for d in range(2):
            ag_copy(d, 1, order(d)[k]).start()
    for h in range(2):
        pt_copy(0, h).start()

    def prepare():
        lax.fori_loop(1, n, w_wait, 0)
        weight = wbuf[...].reshape(n, tokens)
        earlier = lax.broadcasted_iota(jnp.int32, (tokens, tokens), 0) < lax.broadcasted_iota(
            jnp.int32, (tokens, tokens), 1
        )
        earlier = jnp.where(earlier, 1.0, 0.0).astype(jnp.bfloat16)
        chosen = jnp.where(weight > 0.0, 1.0, 0.0).astype(jnp.bfloat16)
        slot_of = jnp.dot(chosen, earlier, preferred_element_type=jnp.float32)
        slot_of = jnp.where(weight > 0.0, slot_of, -1.0)
        for e in range(n):
            slots[e] = slot_of[e : e + 1]
        for load in loads:
            load.wait()

    def y_copy(offset):
        q = chip(offset)
        return pltpu.make_async_remote_copy(
            src_ref=outgo.at[q],
            dst_ref=theirs.at[q],
            send_sem=y_send.at[offset % chips],
            recv_sem=y_recv.at[offset % chips],
            device_id={"ctx": partner},
        )

    def gather(offsets):
        line = lax.broadcasted_iota(jnp.int32, (cap, tokens), 0).astype(jnp.float32)
        for i, offset in enumerate(offsets):
            q = chip(offset)
            for h in range(2):
                pt_copy(offset, h).wait_recv()
            for rel in range(2):
                side = (core + rel) % 2
                j = 2 * i + rel
                hit = jnp.broadcast_to(slots[q * 2 + side], (cap, tokens)) == line
                pick = jnp.where(hit, 1.0, 0.0).astype(jnp.bfloat16)
                place[j] = pick
                scaled = jnp.where(hit, jnp.broadcast_to(wbuf[q * 2 + side], (cap, tokens)), 0.0)
                comb[j] = jnp.broadcast_to(jnp.sum(scaled, axis=1, keepdims=True), (cap, 128))
                for c in range(0, width, 512):
                    rows_in[j * cap : (j + 1) * cap, c : c + 512] = jnp.dot(
                        pick, tok[q, side, :, c : c + 512], preferred_element_type=jnp.float32
                    ).astype(jnp.bfloat16)

    def expand(offsets):
        many_rows = len(offsets) * 2 * cap

        def in_tile(k, _):
            cols = pl.ds(pl.multiple_of(k * 256, 256), 256)
            x = rows_in[:many_rows]
            g = jnp.dot(x, gate_w[:, cols], preferred_element_type=jnp.float32)
            u = jnp.dot(x, up_w[:, cols], preferred_element_type=jnp.float32)
            act[:many_rows, cols] = (g / (1.0 + jnp.exp(-g)) * u).astype(jnp.bfloat16)
            return 0

        lax.fori_loop(0, ff // 256, in_tile, 0)

    def finish(offsets):
        many_rows = len(offsets) * 2 * cap

        def out_tile(k, _):
            cols = pl.ds(pl.multiple_of(k * OUT_TILE, OUT_TILE), OUT_TILE)
            r = jnp.dot(act[:many_rows], down_w[:, cols], preferred_element_type=jnp.float32)
            r = r.astype(jnp.bfloat16).astype(jnp.float32)
            for i, offset in enumerate(offsets):
                for rel, dest in ((0, mine), (1, outgo)):
                    j = 2 * i + rel
                    part = r[j * cap : (j + 1) * cap] * comb[j][:, 0:1]
                    dest[chip(offset), :, cols] = lax.dot_general(
                        place[j],
                        part.astype(jnp.bfloat16),
                        (((0,), (0,)), ((), ())),
                        preferred_element_type=jnp.float32,
                    ).astype(jnp.bfloat16)
            return 0

        lax.fori_loop(0, width // OUT_TILE, out_tile, 0)
        for offset in offsets:
            y_copy(offset).start()

    def relay(step, k):
        for d in range(2):
            h = order(d)[k]
            sign = 1 - 2 * d
            ag_copy(d, step, h).wait_recv()
            if step + 1 < far or (step + 1 == far and k == 0):
                ag_copy(d, step + 1, h).start()
            pt_copy(-sign * step, h).start()

    relay(1, 0)
    prepare()
    relay(1, 1)
    for step in range(1, far):
        pair = (-step, step)
        gather(pair)
        expand(pair)
        relay(step + 1, 0)
        finish(pair)
        if step + 1 < far:
            relay(step + 1, 1)

    def sum_of(q, h):
        return mine[q, rows(h)].astype(jnp.float32) + theirs[q, rows(h)].astype(jnp.float32)

    def rs_copy(d, step, h, src):
        return pltpu.make_async_remote_copy(
            src_ref=src,
            dst_ref=ring_in.at[d, step - 1, h],
            send_sem=rs_send_sem.at[d, step - 1, h],
            recv_sem=rs_recv_sem.at[d, step - 1, h],
            device_id={"ctx": neighbour[d]},
        )

    def rs_step(d, step, k):
        h = order(d)[k]
        sign = 1 - 2 * d
        q = chip(sign * (far + 1 - step))
        if step == 1 or (step == 2 and k == 1):
            mine[q, rows(h)] = sum_of(q, h).astype(jnp.bfloat16)
            src = mine.at[q, rows(h)]
        else:
            src = ring_in.at[d, step - 2, h]
            rs_copy(d, step - 1, h, src).wait_recv()
            ring_in[d, step - 2, h] = (
                ring_in[d, step - 2, h].astype(jnp.float32) + sum_of(q, h)
            ).astype(jnp.bfloat16)
        rs_copy(d, step, h, src).start()

    gather((far,))
    for step in range(1, far):
        for offset in (-step, step):
            y_copy(offset).wait_recv()
    for d in range(2):
        rs_step(d, 2, 1)
    expand((far,))
    finish((far,))
    sends = [(1, 0)]
    for step in range(2, far + 1):
        if step < far:
            sends += [(step + 1, 1)]
        sends += [(step, 0)]
    y_copy(far).wait_recv()
    for i, (step, k) in enumerate(sends):
        for d in range(2):
            rs_step(d, step, k)
        if i == 1:
            gather((0,))
            expand((0,))
        if i == 2:
            finish((0,))
    y_copy(0).wait_recv()
    for h in range(2):
        total = hidden[rows(h)] + sum_of(pos, h)
        for d in range(2):
            rs_copy(d, far, h, ring_in.at[d, far - 1, h]).wait_recv()
            total = total + ring_in[d, far - 1, h].astype(jnp.float32)
        out[rows(h)] = total.astype(jnp.bfloat16)

    for d in range(2):
        for step in range(1, far + 1):
            for k in range(2):
                h = order(d)[k]
                if step < far or k == 0:
                    ag_copy(d, step, h).wait_send()
                if step > 1 or k == 0:
                    rs_copy(d, step, h, ring_in.at[d, step - 1, h]).wait_send()
    for offset in range(chips):
        for h in range(2):
            pt_copy(offset, h).wait_send()
        y_copy(offset).wait_send()


    for p in range(passes):
        for d in range(2):
            for step in range(1, far + 1):
                for k in range(2):
                    if step < far or k == 0:
                        wg_copy(d, step, p, order(d)[k]).wait_send()
        wp_copy(p).wait_send()
        for kind in range(3):
            h_copy(kind, p).wait_send()
    for g in range(KVH):
        for kind in range(3):
            at_copy(kind, g).wait_send()


def write_kernel(a, b, a_out, b_out, sem):
    copies = [
        pltpu.make_async_copy(x, y, sem.at[k]) for k, (x, y) in enumerate(((a, a_out), (b, b_out)))
    ]
    for copy in copies:
        copy.start()
    for copy in copies:
        copy.wait()


def layer_ring(
    queries,
    keys,
    values,
    block_ids,
    out_weight,
    summary_gain,
    norm_gain,
    routes,
    route_scores,
    expert_gate,
    expert_up,
    expert_down,
    n,
    cap,
):
    tokens, width = queries.shape
    ff = expert_gate.shape[-1]
    chips = n // 2
    far = chips // 2
    vmem = pl.BlockSpec(memory_space=pltpu.VMEM)
    hbm = pl.BlockSpec(memory_space=pl.ANY)
    dma = pltpu.SemaphoreType.DMA
    bf16, f32 = jnp.bfloat16, jnp.float32
    result = jax.ShapeDtypeStruct((tokens, width), bf16)
    pair = pl.pallas_call(
        functools.partial(layer_kernel, n, cap),
        out_shape=(result, result),
        in_specs=[vmem] * 9 + [hbm] * 3,
        out_specs=(vmem, vmem),
        scratch_shapes=[
            pltpu.VMEM((tokens, width), bf16),
            pltpu.VMEM((tokens, width), f32),
            pltpu.VMEM((4 * tokens, width), bf16),
            pltpu.VMEM((PASSES, chips, 2 * out_weight.shape[0], width // (4 * PASSES)), bf16),
            pltpu.VMEM((PASSES, 4, tokens, width // (4 * PASSES)), bf16),
            pltpu.VMEM((4, PASSES, tokens, width // (4 * PASSES)), bf16),
            pltpu.VMEM((2 * NB, KVH * HD), bf16),
            pltpu.VMEM((n, 2 * NB, KVH * HD), bf16),
            pltpu.VMEM((n, 1, tokens), f32),
            pltpu.VMEM((width, ff), bf16),
            pltpu.VMEM((width, ff), bf16),
            pltpu.VMEM((ff, width), bf16),
            pltpu.VMEM((chips, 2, tokens, width), bf16),
            pltpu.VMEM((n, 1, tokens), f32),
            pltpu.VMEM((n, 1, tokens), f32),
            pltpu.VMEM((4 * cap, width), bf16),
            pltpu.VMEM((4 * cap, ff), bf16),
            pltpu.VMEM((4, cap, tokens), bf16),
            pltpu.VMEM((4, cap, 128), f32),
            pltpu.VMEM((chips, tokens, width), bf16),
            pltpu.VMEM((chips, tokens, width), bf16),
            pltpu.VMEM((chips, tokens, width), bf16),
            pltpu.VMEM((2, far, 2, tokens // 2, width), bf16),
            dma((3,)),
            dma((n,)),
            dma((n,)),
            dma((2, far, PASSES, 2)),
            dma((2, far, PASSES, 2)),
            dma((PASSES,)),
            dma((PASSES,)),
            dma((3, KVH)),
            dma((3, KVH)),
            dma((3, PASSES)),
            dma((3, PASSES)),
            dma((n,)),
            dma((n,)),
            dma((2, far, 2)),
            dma((2, far, 2)),
            dma((chips, 2)),
            dma((chips, 2)),
            dma((chips,)),
            dma((chips,)),
            dma((2, far, 2)),
            dma((2, far, 2)),
        ],
        compiler_params=pltpu.CompilerParams(
            collective_id=1, has_side_effects=True, vmem_limit_bytes=62 * 2**20
        ),
    )(
        queries,
        keys,
        values,
        block_ids[None, :],
        out_weight,
        summary_gain[None, :],
        norm_gain[None, :],
        routes.T,
        route_scores.T,
        expert_gate[0],
        expert_up[0],
        expert_down[0],
    )
    return pl.pallas_call(
        write_kernel,
        out_shape=(result, result),
        in_specs=[vmem] * 2,
        out_specs=(hbm, hbm),
        scratch_shapes=[dma((2,))],
    )(*pair)


def body(
    queries,
    keys,
    values,
    block_ids,
    out_weight,
    summary_gain,
    norm_gain,
    routes,
    route_scores,
    expert_gate,
    expert_up,
    expert_down,
):
    tokens_here = queries.shape[0]
    combine = route_scores / jnp.sum(route_scores, axis=-1, keepdims=True)
    experts_all = EXP_DEV * lax.axis_size("ctx")
    capacity = max(2, 5 * tokens_here * TOP // (4 * experts_all))
    chips = experts_all // 2
    fits = experts_all * tokens_here * D * 2 <= RING_BYTES
    if fits and chips % 4 == 0 and lax.axis_size("groups") == 2:
        return layer_ring(
            queries,
            keys,
            values,
            block_ids,
            out_weight,
            summary_gain,
            norm_gain,
            routes,
            route_scores,
            expert_gate,
            expert_up,
            expert_down,
            experts_all,
            -(-capacity // 16) * 16,
        )
    group = HQ // KVH
    scale = 1.0 / math.sqrt(HD)
    member = block_ids[None, :] == jnp.arange(NB, dtype=jnp.int32)[:, None]
    count = jnp.sum(member.astype(jnp.float32), axis=-1)
    indicator = member.astype(jnp.bfloat16)
    kmean = jnp.dot(indicator, keys, preferred_element_type=jnp.float32) / count[:, None]
    vmean = jnp.dot(indicator, values, preferred_element_type=jnp.float32) / count[:, None]
    summary_keys = (
        (normalize(kmean.reshape(NB, KVH, HD)) * summary_gain)
        .astype(jnp.bfloat16)
        .reshape(NB, KVH * HD)
    )
    summary_values = (
        normalize(vmean.reshape(NB, KVH, HD)).astype(jnp.bfloat16).reshape(NB, KVH * HD)
    )
    summaries = lax.all_gather(
        jnp.concatenate([summary_keys, summary_values], axis=1), "ctx", axis=0, tiled=True
    )
    all_keys, all_values = summaries[:, : KVH * HD], summaries[:, KVH * HD :]
    index = lax.axis_index("ctx")
    query = queries.reshape(tokens_here, KVH, group, HD)
    key_loc = keys.reshape(tokens_here, KVH, HD)
    remote_keys = all_keys.reshape(-1, KVH, HD)
    causal = jnp.arange(tokens_here)[:, None] >= jnp.arange(tokens_here)[None, :]
    owner = jnp.arange(remote_keys.shape[0], dtype=jnp.int32) // NB
    local = jnp.einsum("tkgd,skd->kgts", query, key_loc, preferred_element_type=jnp.float32) * scale
    local = jnp.where(causal[None, None], local, -jnp.inf)
    remote = (
        jnp.einsum("tkgd,skd->kgts", query, remote_keys, preferred_element_type=jnp.float32) * scale
    )
    remote = jnp.where((owner < index)[None, None, None, :], remote, -jnp.inf)
    scores = jnp.concatenate([local, remote], axis=-1)
    top = jnp.max(scores, axis=-1, keepdims=True)
    expo = jnp.exp(scores - top)
    weights = (expo / jnp.sum(expo, axis=-1, keepdims=True)).astype(jnp.bfloat16)
    every_value = jnp.concatenate(
        [values.reshape(tokens_here, KVH, HD), all_values.reshape(-1, KVH, HD)], axis=0
    )
    attended = jnp.einsum(
        "kgts,skd->tkgd", weights, every_value, preferred_element_type=jnp.float32
    )
    attended = attended.reshape(tokens_here, HQ * HD).astype(jnp.bfloat16)
    hidden = jnp.dot(
        attended,
        lax.all_gather(out_weight, "ctx", axis=0, tiled=True),
        preferred_element_type=jnp.float32,
    )
    normed = (normalize(hidden) * norm_gain).astype(jnp.bfloat16)
    flat_routes = routes.reshape(-1)
    hits = (flat_routes[:, None] == jnp.arange(experts_all, dtype=jnp.int32)[None, :]).astype(
        jnp.int32
    )
    slot = jnp.sum(hits * (jnp.cumsum(hits, axis=0) - 1), axis=-1)
    target = flat_routes * capacity + slot
    source = jnp.arange(tokens_here * TOP, dtype=jnp.int32) // TOP
    outgoing = jnp.zeros((experts_all * capacity, D), jnp.bfloat16).at[target].set(normed[source])
    outgoing = outgoing.reshape(experts_all, capacity, D)
    arrived = lax.all_to_all(outgoing, "ctx", split_axis=0, concat_axis=0, tiled=True)
    senders = arrived.shape[0] // EXP_DEV
    width = arrived.shape[1]
    inputs = (
        arrived.reshape(senders, EXP_DEV, width, D)
        .transpose(1, 0, 2, 3)
        .reshape(EXP_DEV, senders * width, D)
    )
    gate = jnp.einsum("erd,edf->erf", inputs, expert_gate, preferred_element_type=jnp.float32)
    upper = jnp.einsum("erd,edf->erf", inputs, expert_up, preferred_element_type=jnp.float32)
    act = (jax.nn.silu(gate) * upper).astype(jnp.bfloat16)
    result = jnp.einsum(
        "erf,efd->erd", act, expert_down, preferred_element_type=jnp.float32
    ).astype(jnp.bfloat16)
    result = (
        result.reshape(EXP_DEV, senders, width, D)
        .transpose(1, 0, 2, 3)
        .reshape(senders * EXP_DEV, width, D)
    )
    returned = lax.all_to_all(result, "ctx", split_axis=0, concat_axis=0, tiled=True)
    returned = returned.reshape(experts_all * capacity, D)
    picked = jnp.take(returned, target, axis=0).reshape(tokens_here, TOP, D)
    blended = jnp.sum(combine[:, :, None] * picked.astype(jnp.float32), axis=1)
    return (hidden.astype(jnp.bfloat16), (hidden + blended).astype(jnp.bfloat16))


def solution(mesh):
    in_specs = (
        P(("groups", "ctx"), None),
        P(("groups", "ctx"), None),
        P(("groups", "ctx"), None),
        P(("groups", "ctx")),
        P("ctx", None),
        P(),
        P(),
        P(("groups", "ctx"), None),
        P(("groups", "ctx"), None),
        P("ctx", None, None),
        P("ctx", None, None),
        P("ctx", None, None),
    )
    out_specs = (P(("groups", "ctx"), None), P(("groups", "ctx"), None))
    return jax.shard_map(body, mesh=mesh, in_specs=in_specs, out_specs=out_specs, check_vma=False)
```

```python
import functools
import math

import jax
import jax.numpy as jnp
from jax import lax
from jax.experimental import pallas as pl
from jax.experimental.pallas import tpu as pltpu
from jax.sharding import PartitionSpec as P

D = 2048
HQ = 16
KVH = 4
HD = 128
TOP = 8
EXP_DEV = 1
NB = 4


def normalize(x):
    return x * lax.rsqrt(jnp.mean(x * x, axis=-1, keepdims=True) + 1e-06)


RING_BYTES = 16 * 2**20
PASSES = 2
PARTS = 2


def chip_at(position, chips):
    depth = chips // 2
    y = position // depth
    return (position * (1 - y) + (chips - 1 - position) * y) * 2 + y


def layer_kernel(
    n,
    cap,
    queries,
    keys,
    values,
    blocks,
    weight_own,
    key_gain,
    norm_gain,
    routes,
    route_scores,
    gate_hbm,
    up_hbm,
    down_hbm,
    projected,
    out,
    normed,
    hidden,
    att,
    wq,
    outq,
    hidq,
    sums_own,
    sums,
    share,
    gate_w,
    up_w,
    down_w,
    tok,
    wbuf,
    slots,
    rows_in,
    act,
    place,
    comb,
    results,
    theirs,
    ring_in,
    load_sem,
    s_send,
    s_recv,
    wg_send,
    wg_recv,
    wp_send,
    wp_recv,
    at_send,
    at_recv,
    h_send,
    h_recv,
    w_send,
    w_recv,
    ag_send,
    ag_recv,
    pt_send,
    pt_recv,
    y_send,
    y_recv,
    rs_send_sem,
    rs_recv_sem,
):
    tokens = normed.shape[0]
    half = tokens // 2
    width = normed.shape[1]
    ff = gate_w.shape[1]
    chips = n // 2
    far = chips // 2
    me = lax.axis_index("ctx")
    core = me % 2
    y = (me // 2) % 2
    z = me // 4
    pos = z * (1 - y) + (chips - 1 - z) * y
    partner = me + 1 - 2 * core
    ahead = chip_at((pos + 1) % chips, chips) * 2 + core
    behind = chip_at((pos + chips - 1) % chips, chips) * 2 + core
    neighbour = (ahead, behind)

    loads = [
        pltpu.make_async_copy(a, b, load_sem.at[k])
        for k, (a, b) in enumerate(((gate_hbm, gate_w), (up_hbm, up_w), (down_hbm, down_w)))
    ]
    for load in loads:
        load.start()

    barrier = pltpu.get_barrier_semaphore()
    across = 1 - lax.axis_index("groups")

    def greet(k, _):
        pl.semaphore_signal(barrier, inc=1, device_id={"ctx": (me + k) % n})
        return 0

    lax.fori_loop(1, n, greet, 0)
    pl.semaphore_signal(barrier, inc=1, device_id={"groups": across})
    pl.semaphore_signal(barrier, inc=1, device_id={"groups": across, "ctx": partner})

    def mean_of(ref):
        shape = (2 * NB, tokens)
        ids = jnp.broadcast_to(blocks[...], shape)
        member = jnp.where(ids == lax.broadcasted_iota(jnp.int32, shape, 0) % NB, 1.0, 0.0)
        count = jnp.sum(member, axis=1, keepdims=True)
        return (
            jnp.dot(member.astype(jnp.bfloat16), ref[...], preferred_element_type=jnp.float32)
            / count
        )

    kmean, vmean = mean_of(keys), mean_of(values)
    upper = lax.broadcasted_iota(jnp.int32, (2 * NB, HD), 0) < NB
    for g in range(KVH):
        cols = slice(g * HD, (g + 1) * HD)
        sums_own[:, cols] = jnp.where(
            upper, normalize(kmean[:, cols]) * key_gain[...], normalize(vmean[:, cols])
        ).astype(jnp.bfloat16)
    pl.semaphore_wait(barrier, n + 1)

    def s_copy(k):
        return pltpu.make_async_remote_copy(
            src_ref=sums_own,
            dst_ref=sums.at[me],
            send_sem=s_send.at[k],
            recv_sem=s_recv.at[k],
            device_id={"ctx": (me + 2 * k) % n},
        )

    def sp_copy(k):
        source = (me + n - 2 * k) % n
        return pltpu.make_async_remote_copy(
            src_ref=sums.at[source],
            dst_ref=sums.at[source],
            send_sem=s_send.at[chips + k],
            recv_sem=s_recv.at[chips + k],
            device_id={"ctx": partner},
        )

    own_copy = pltpu.make_async_remote_copy(
        src_ref=sums_own,
        dst_ref=sums.at[me],
        send_sem=s_send.at[chips],
        recv_sem=s_recv.at[chips],
        device_id={"ctx": partner},
    )

    def s_start(k, _):
        s_copy(k).start()
        return 0

    def s_pass(k, _):
        s_copy(k).wait_recv()
        sp_copy(k).start()
        return 0

    def s_wait(k, _):
        sp_copy(k).wait_recv()
        s_copy(k).wait_send()
        sp_copy(k).wait_send()
        return 0

    lax.fori_loop(1, chips, s_start, 0)
    own_copy.start()
    sums[me] = sums_own[...]

    def rows(h):
        return pl.ds(h * half, half)

    def chip(offset):
        return (pos + offset + chips) % chips

    def ag_copy(d, step, h):
        sign = 1 - 2 * d
        q = chip(-sign * (step - 1))
        src = normed.at[rows(h)] if step == 1 else tok.at[q, core, rows(h)]
        return pltpu.make_async_remote_copy(
            src_ref=src,
            dst_ref=tok.at[q, core, rows(h)],
            send_sem=ag_send.at[d, step - 1, h],
            recv_sem=ag_recv.at[d, step - 1, h],
            device_id={"ctx": neighbour[d]},
        )

    def pt_copy(offset, h):
        q = chip(offset)
        src = normed.at[rows(h)] if offset == 0 else tok.at[q, core, rows(h)]
        return pltpu.make_async_remote_copy(
            src_ref=src,
            dst_ref=tok.at[q, core, rows(h)],
            send_sem=pt_send.at[offset % chips, h],
            recv_sem=pt_recv.at[offset % chips, h],
            device_id={"ctx": partner},
        )

    def order(d):
        return (0, 1) if d == 0 else (1, 0)

    wrows = weight_own.shape[0]
    passes, pcols = wq.shape[0], wq.shape[3]
    group = 1 - across
    slot = group * 2 + core

    def own_rows(t):
        return pl.ds(pl.multiple_of((core if t == 0 else 1 - core) * wrows, wrows), wrows)

    def w_cols(t, p):
        side = group * 2 + (core if t == 0 else 1 - core)
        return pl.ds(pl.multiple_of((side * passes + p) * pcols, pcols), pcols)

    def w_at(p, q, t):
        return wq.at[p, chip_at(q, chips), own_rows(t)]

    def wg_copy(d, step, p, t):
        sign = 1 - 2 * d
        if step == 1:
            src, dst = weight_own.at[:, w_cols(t, p)], w_at(p, pos, 0)
            target = neighbour[d] + t * (1 - 2 * core)
        else:
            src = dst = w_at(p, chip(-sign * (step - 1)), t)
            target = neighbour[d]
        return pltpu.make_async_remote_copy(
            src_ref=src,
            dst_ref=dst,
            send_sem=wg_send.at[d, step - 1, p, t],
            recv_sem=wg_recv.at[d, step - 1, p, t],
            device_id={"ctx": target},
        )

    def wp_copy(p):
        return pltpu.make_async_remote_copy(
            src_ref=weight_own.at[:, w_cols(1, p)],
            dst_ref=w_at(p, pos, 0),
            send_sem=wp_send.at[p],
            recv_sem=wp_recv.at[p],
            device_id={"ctx": partner},
        )

    def at_copy(kind, g):
        span = HQ // KVH * HD
        source = slot if kind < 2 else across * 2 + core
        block = att.at[
            pl.ds(pl.multiple_of(source * tokens, tokens), tokens), g * span : (g + 1) * span
        ]
        return pltpu.make_async_remote_copy(
            src_ref=block,
            dst_ref=block,
            send_sem=at_send.at[kind, g],
            recv_sem=at_recv.at[kind, g],
            device_id={"groups": across} if kind == 1 else {"ctx": partner},
        )

    def h_copy(kind, p):
        target = (
            {"ctx": partner},
            {"groups": across},
            {"groups": across, "ctx": partner},
        )[kind]
        theirs_slot = (group, across, across)[kind] * 2 + (1 - core, core, 1 - core)[kind]
        return pltpu.make_async_remote_copy(
            src_ref=outq.at[p, theirs_slot],
            dst_ref=hidq.at[slot, p],
            send_sem=h_send.at[kind, p],
            recv_sem=h_recv.at[kind, p],
            device_id=target,
        )

    for p in range(passes):
        for k in range(2):
            for d in range(2):
                wg_copy(d, 1, p, order(d)[k]).start()
    for p in range(passes):
        wp_copy(p).start()
        wq[p, chip_at(pos, chips), own_rows(0)] = weight_own[:, w_cols(0, p)]

    def w_copy(k):
        target = (me + k) % n
        return pltpu.make_async_remote_copy(
            src_ref=share.at[target],
            dst_ref=wbuf.at[pos * 2 + core],
            send_sem=w_send.at[k],
            recv_sem=w_recv.at[k],
            device_id={"ctx": target},
        )

    def w_start(k, _):
        w_copy(k).start()
        return 0

    def w_wait(k, _):
        w_copy(k).wait()
        return 0

    chosen_scores = route_scores[...]
    combine = chosen_scores / jnp.sum(chosen_scores, axis=0, keepdims=True)
    expert = lax.broadcasted_iota(jnp.int32, (n, tokens), 0)
    table_of = jnp.zeros((n, tokens), jnp.float32)
    for c in range(TOP):
        table_of = table_of + jnp.where(routes[c : c + 1] == expert, combine[c : c + 1], 0.0)
    for e in range(n):
        share[e] = table_of[e : e + 1]
    lax.fori_loop(1, n, w_start, 0)
    wbuf[pos * 2 + core] = share[me]
    lax.fori_loop(1, chips, s_pass, 0)
    own_copy.wait()
    lax.fori_loop(1, chips, s_wait, 0)

    many = HQ // KVH
    scale = 1.0 / math.sqrt(HD)
    tall = (many * tokens, tokens)
    causal = lax.broadcasted_iota(jnp.int32, tall, 0) % tokens >= lax.broadcasted_iota(
        jnp.int32, tall, 1
    )
    far_shape = (many * tokens, n * 2 * NB)
    entry = lax.broadcasted_iota(jnp.int32, far_shape, 1)
    seen = (entry % (2 * NB) < NB) & (entry // (2 * NB) < me)
    contract_last = (((1,), (1,)), ((), ()))

    def attend(g):
        cols = slice(g * HD, (g + 1) * HD)
        heads = [slice((g * many + i) * HD, (g * many + i + 1) * HD) for i in range(many)]
        q = jnp.concatenate([queries[:, c] for c in heads], axis=0)
        table = sums[:, :, cols].astype(jnp.float32).reshape(n * 2 * NB, HD)
        shifted = jnp.concatenate([table[NB:], table[:NB]], axis=0).astype(jnp.bfloat16)
        table = table.astype(jnp.bfloat16)
        near = (
            lax.dot_general(q, keys[:, cols], contract_last, preferred_element_type=jnp.float32)
            * scale
        )
        near = jnp.where(causal, near, -jnp.inf)
        remote = lax.dot_general(q, table, contract_last, preferred_element_type=jnp.float32) * scale
        remote = jnp.where(seen, remote, -jnp.inf)
        top = jnp.maximum(
            jnp.max(near, axis=1, keepdims=True), jnp.max(remote, axis=1, keepdims=True)
        )
        near, remote = jnp.exp(near - top), jnp.exp(remote - top)
        total = jnp.sum(near, axis=1, keepdims=True) + jnp.sum(remote, axis=1, keepdims=True)
        near, remote = (near / total).astype(jnp.bfloat16), (remote / total).astype(jnp.bfloat16)
        result = jnp.dot(
            near, values[:, cols], preferred_element_type=jnp.float32
        ) + jnp.dot(remote, shifted, preferred_element_type=jnp.float32)
        result = result.astype(jnp.bfloat16)
        for i, c in enumerate(heads):
            att[pl.ds(pl.multiple_of(slot * tokens, tokens), tokens), c] = result[
                i * tokens : (i + 1) * tokens
            ]
        at_copy(1, g).start()
        at_copy(0, g).start()

    def project(p):
        weight = wq[p].reshape(chips * 2 * wrows, pcols)
        for side in (across, group):
            left = att[pl.ds(pl.multiple_of(side * 2 * tokens, 2 * tokens), 2 * tokens)]
            part = jnp.dot(left, weight, preferred_element_type=jnp.float32).astype(jnp.bfloat16)
            for c in range(2):
                outq[p, side * 2 + c] = part[c * tokens : (c + 1) * tokens]
            if side is across:
                h_copy(1, p).start()
                h_copy(2, p).start()
            else:
                h_copy(0, p).start()
        hidq[slot, p] = outq[p, slot]

    def w_step(step, p):
        for k in range(2):
            for d in range(2):
                t = order(d)[k]
                if step < far or k == 0:
                    wg_copy(d, step, p, t).wait_recv()
                if step + 1 < far or (step + 1 == far and k == 0):
                    wg_copy(d, step + 1, p, t).start()

    for g in range(KVH):
        attend(g)
        if g > 0:
            at_copy(1, g - 1).wait_recv()
            at_copy(2, g - 1).start()
        if g + 1 < far:
            for p in range(passes):
                w_step(g + 1, p)
    at_copy(1, KVH - 1).wait_recv()
    at_copy(2, KVH - 1).start()
    for p in range(passes):
        wp_copy(p).wait_recv()
    for g in range(KVH):
        at_copy(0, g).wait_recv()
        at_copy(2, g).wait_recv()
    for p in range(passes):
        for step in range(min(KVH + 1, far), far + 1):
            w_step(step, p)
        project(p)
    for p in range(passes):
        for kind in range(3):
            h_copy(kind, p).wait_recv()
        for s in range(4):
            at = (s * passes + p) * pcols
            hidden[:, at : at + pcols] = hidq[s, p].astype(jnp.float32)
    for h in range(2):
        hid = hidden[rows(h)]
        projected[rows(h)] = hid.astype(jnp.bfloat16)
        tidy = (normalize(hid) * norm_gain[...]).astype(jnp.bfloat16)
        normed[rows(h)] = tidy
        tok[pos, core, rows(h)] = tidy

    for k in range(2):
        for d in range(2):
            ag_copy(d, 1, order(d)[k]).start()
    for h in range(2):
        pt_copy(0, h).start()

    def prepare():
        lax.fori_loop(1, n, w_wait, 0)
        weight = wbuf[...].reshape(n, tokens)
        earlier = lax.broadcasted_iota(jnp.int32, (tokens, tokens), 0) < lax.broadcasted_iota(
            jnp.int32, (tokens, tokens), 1
        )
        earlier = jnp.where(earlier, 1.0, 0.0).astype(jnp.bfloat16)
        chosen = jnp.where(weight > 0.0, 1.0, 0.0).astype(jnp.bfloat16)
        slot_of = jnp.dot(chosen, earlier, preferred_element_type=jnp.float32)
        slot_of = jnp.where(weight > 0.0, slot_of, -1.0)
        for e in range(n):
            slots[e] = slot_of[e : e + 1]
        place[...] = jnp.zeros_like(place)
        for load in loads:
            load.wait()

    part_width = width // PARTS

    def cols_of(c):
        return slice(c * part_width, (c + 1) * part_width)

    def y_copy(offset, c):
        q = chip(offset)
        return pltpu.make_async_remote_copy(
            src_ref=results.at[q, 1 - core, :, cols_of(c)],
            dst_ref=theirs.at[q, :, cols_of(c)],
            send_sem=y_send.at[offset % chips, c],
            recv_sem=y_recv.at[offset % chips, c],
            device_id={"ctx": partner},
        )

    def gather(offsets):
        line = lax.broadcasted_iota(jnp.int32, (cap, tokens), 0).astype(jnp.float32)
        for i, offset in enumerate(offsets):
            q = chip(offset)
            for side in range(2):
                hit = jnp.broadcast_to(slots[q * 2 + side], (cap, tokens)) == line
                pick = jnp.where(hit, 1.0, 0.0).astype(jnp.bfloat16)
                span = slice(side * cap, (side + 1) * cap)
                place[i, span, side * tokens : (side + 1) * tokens] = pick
                scaled = jnp.where(hit, jnp.broadcast_to(wbuf[q * 2 + side], (cap, tokens)), 0.0)
                comb[i, span] = jnp.broadcast_to(
                    jnp.sum(scaled, axis=1, keepdims=True), (cap, 128)
                )
        for i, offset in enumerate(offsets):
            q = chip(offset)
            for h in range(2):
                pt_copy(offset, h).wait_recv()
            for c in range(0, width, 512):
                rows_in[i * 2 * cap : (i + 1) * 2 * cap, c : c + 512] = jnp.dot(
                    place[i],
                    tok[q, :, :, c : c + 512].reshape(2 * tokens, 512),
                    preferred_element_type=jnp.float32,
                ).astype(jnp.bfloat16)

    def expand(offsets):
        many_rows = len(offsets) * 2 * cap

        def in_tile(k, _):
            cols = pl.ds(pl.multiple_of(k * 256, 256), 256)
            x = rows_in[:many_rows]
            g = jnp.dot(x, gate_w[:, cols], preferred_element_type=jnp.float32)
            u = jnp.dot(x, up_w[:, cols], preferred_element_type=jnp.float32)
            act[:many_rows, cols] = (g / (1.0 + jnp.exp(-g)) * u).astype(jnp.bfloat16)
            return 0

        lax.fori_loop(0, ff // 256, in_tile, 0)

    def finish(offsets):
        many_rows = len(offsets) * 2 * cap
        for c in range(PARTS):
            r = jnp.dot(
                act[:many_rows], down_w[:, cols_of(c)], preferred_element_type=jnp.float32
            )
            r = r.astype(jnp.bfloat16).astype(jnp.float32)
            for i, offset in enumerate(offsets):
                part = r[i * 2 * cap : (i + 1) * 2 * cap] * comb[i][:, 0:1]
                spread = lax.dot_general(
                    place[i],
                    part.astype(jnp.bfloat16),
                    (((0,), (0,)), ((), ())),
                    preferred_element_type=jnp.float32,
                ).astype(jnp.bfloat16)
                for side in range(2):
                    results[chip(offset), side, :, cols_of(c)] = spread[
                        side * tokens : (side + 1) * tokens
                    ]
            for offset in offsets:
                y_copy(offset, c).start()

    def relay(step, k):
        for d in range(2):
            h = order(d)[k]
            sign = 1 - 2 * d
            ag_copy(d, step, h).wait_recv()
            if step + 1 < far or (step + 1 == far and k == 0):
                ag_copy(d, step + 1, h).start()
            pt_copy(-sign * step, h).start()

    relay(1, 0)
    prepare()
    relay(1, 1)
    for step in range(1, far):
        pair = (-step, step)
        gather(pair)
        expand(pair)
        if step + 1 < far:
            relay(step + 1, 0)
        finish(pair)
        if step + 1 < far:
            relay(step + 1, 1)

    def sum_of(q, h, c):
        own = results[q, core, rows(h), cols_of(c)].astype(jnp.float32)
        return own + theirs[q, rows(h), cols_of(c)].astype(jnp.float32)

    def rs_copy(d, step, h, c, src):
        return pltpu.make_async_remote_copy(
            src_ref=src,
            dst_ref=ring_in.at[d, step - 1, h, :, cols_of(c)],
            send_sem=rs_send_sem.at[d, step - 1, h, c],
            recv_sem=rs_recv_sem.at[d, step - 1, h, c],
            device_id={"ctx": neighbour[d]},
        )

    def landed(d, step, h, c):
        return ring_in.at[d, step - 1, h, :, cols_of(c)]

    def rs_part(d, step, k, c):
        h = order(d)[k]
        sign = 1 - 2 * d
        q = chip(sign * (far + 1 - step))
        if step == 1 or (step == 2 and k == 1):
            results[q, core, rows(h), cols_of(c)] = sum_of(q, h, c).astype(jnp.bfloat16)
            src = results.at[q, core, rows(h), cols_of(c)]
        else:
            src = landed(d, step - 1, h, c)
            rs_copy(d, step - 1, h, c, src).wait_recv()
            ring_in[d, step - 2, h, :, cols_of(c)] = (
                ring_in[d, step - 2, h, :, cols_of(c)].astype(jnp.float32) + sum_of(q, h, c)
            ).astype(jnp.bfloat16)
        rs_copy(d, step, h, c, src).start()

    def rs_step(step, k):
        for c in range(PARTS):
            for d in range(2):
                rs_part(d, step, k, c)

    for step in range(1, far - 1):
        for offset in (-step, step):
            for c in range(PARTS):
                y_copy(offset, c).wait_recv()
    for c in range(PARTS):
        for d in range(2):
            y_copy((1 - 2 * d) * (far - 1), c).wait_recv()
            rs_part(d, 2, 1, c)
    relay(far, 0)
    gather((far,))
    expand((far,))
    finish((far,))
    for c in range(PARTS):
        y_copy(far, c).wait_recv()
        for d in range(2):
            rs_part(d, 1, 0, c)
    for step in range(2, far + 1):
        if step < far:
            rs_step(step + 1, 1)
        if step == 2:
            gather((0,))
            expand((0,))
        rs_step(step, 0)
        if step == 2:
            finish((0,))
    for c in range(PARTS):
        y_copy(0, c).wait_recv()
    for c in range(PARTS):
        for h in range(2):
            total = hidden[rows(h), cols_of(c)] + sum_of(pos, h, c)
            for d in range(2):
                rs_copy(d, far, h, c, landed(d, far, h, c)).wait_recv()
                total = total + ring_in[d, far - 1, h, :, cols_of(c)].astype(jnp.float32)
            out[rows(h), cols_of(c)] = total.astype(jnp.bfloat16)

    for d in range(2):
        for step in range(1, far + 1):
            for k in range(2):
                h = order(d)[k]
                if step < far or k == 0:
                    ag_copy(d, step, h).wait_send()
                if step > 1 or k == 0:
                    for c in range(PARTS):
                        rs_copy(d, step, h, c, landed(d, step, h, c)).wait_send()
    for offset in range(chips):
        for h in range(2):
            pt_copy(offset, h).wait_send()
        for c in range(PARTS):
            y_copy(offset, c).wait_send()


    for p in range(passes):
        for d in range(2):
            for step in range(1, far + 1):
                for k in range(2):
                    if step < far or k == 0:
                        wg_copy(d, step, p, order(d)[k]).wait_send()
        wp_copy(p).wait_send()
        for kind in range(3):
            h_copy(kind, p).wait_send()
    for g in range(KVH):
        for kind in range(3):
            at_copy(kind, g).wait_send()


def write_kernel(a, b, a_out, b_out, sem):
    copies = [
        pltpu.make_async_copy(x, y, sem.at[k]) for k, (x, y) in enumerate(((a, a_out), (b, b_out)))
    ]
    for copy in copies:
        copy.start()
    for copy in copies:
        copy.wait()


def layer_ring(
    queries,
    keys,
    values,
    block_ids,
    out_weight,
    summary_gain,
    norm_gain,
    routes,
    route_scores,
    expert_gate,
    expert_up,
    expert_down,
    n,
    cap,
):
    tokens, width = queries.shape
    ff = expert_gate.shape[-1]
    chips = n // 2
    far = chips // 2
    vmem = pl.BlockSpec(memory_space=pltpu.VMEM)
    hbm = pl.BlockSpec(memory_space=pl.ANY)
    dma = pltpu.SemaphoreType.DMA
    bf16, f32 = jnp.bfloat16, jnp.float32
    result = jax.ShapeDtypeStruct((tokens, width), bf16)
    pair = pl.pallas_call(
        functools.partial(layer_kernel, n, cap),
        out_shape=(result, result),
        in_specs=[vmem] * 9 + [hbm] * 3,
        out_specs=(vmem, vmem),
        scratch_shapes=[
            pltpu.VMEM((tokens, width), bf16),
            pltpu.VMEM((tokens, width), f32),
            pltpu.VMEM((4 * tokens, width), bf16),
            pltpu.VMEM((PASSES, chips, 2 * out_weight.shape[0], width // (4 * PASSES)), bf16),
            pltpu.VMEM((PASSES, 4, tokens, width // (4 * PASSES)), bf16),
            pltpu.VMEM((4, PASSES, tokens, width // (4 * PASSES)), bf16),
            pltpu.VMEM((2 * NB, KVH * HD), bf16),
            pltpu.VMEM((n, 2 * NB, KVH * HD), bf16),
            pltpu.VMEM((n, 1, tokens), f32),
            pltpu.VMEM((width, ff), bf16),
            pltpu.VMEM((width, ff), bf16),
            pltpu.VMEM((ff, width), bf16),
            pltpu.VMEM((chips, 2, tokens, width), bf16),
            pltpu.VMEM((n, 1, tokens), f32),
            pltpu.VMEM((n, 1, tokens), f32),
            pltpu.VMEM((4 * cap, width), bf16),
            pltpu.VMEM((4 * cap, ff), bf16),
            pltpu.VMEM((2, 2 * cap, 2 * tokens), bf16),
            pltpu.VMEM((2, 2 * cap, 128), f32),
            pltpu.VMEM((chips, 2, tokens, width), bf16),
            pltpu.VMEM((chips, tokens, width), bf16),
            pltpu.VMEM((2, far, 2, tokens // 2, width), bf16),
            dma((3,)),
            dma((n,)),
            dma((n,)),
            dma((2, far, PASSES, 2)),
            dma((2, far, PASSES, 2)),
            dma((PASSES,)),
            dma((PASSES,)),
            dma((3, KVH)),
            dma((3, KVH)),
            dma((3, PASSES)),
            dma((3, PASSES)),
            dma((n,)),
            dma((n,)),
            dma((2, far, 2)),
            dma((2, far, 2)),
            dma((chips, 2)),
            dma((chips, 2)),
            dma((chips, PARTS)),
            dma((chips, PARTS)),
            dma((2, far, 2, PARTS)),
            dma((2, far, 2, PARTS)),
        ],
        compiler_params=pltpu.CompilerParams(
            collective_id=1, has_side_effects=True, vmem_limit_bytes=62 * 2**20
        ),
    )(
        queries,
        keys,
        values,
        block_ids[None, :],
        out_weight,
        summary_gain[None, :],
        norm_gain[None, :],
        routes.T,
        route_scores.T,
        expert_gate[0],
        expert_up[0],
        expert_down[0],
    )
    return pl.pallas_call(
        write_kernel,
        out_shape=(result, result),
        in_specs=[vmem] * 2,
        out_specs=(hbm, hbm),
        scratch_shapes=[dma((2,))],
    )(*pair)


def body(
    queries,
    keys,
    values,
    block_ids,
    out_weight,
    summary_gain,
    norm_gain,
    routes,
    route_scores,
    expert_gate,
    expert_up,
    expert_down,
):
    tokens_here = queries.shape[0]
    combine = route_scores / jnp.sum(route_scores, axis=-1, keepdims=True)
    experts_all = EXP_DEV * lax.axis_size("ctx")
    capacity = max(2, 5 * tokens_here * TOP // (4 * experts_all))
    chips = experts_all // 2
    fits = experts_all * tokens_here * D * 2 <= RING_BYTES
    if fits and chips % 4 == 0 and lax.axis_size("groups") == 2:
        return layer_ring(
            queries,
            keys,
            values,
            block_ids,
            out_weight,
            summary_gain,
            norm_gain,
            routes,
            route_scores,
            expert_gate,
            expert_up,
            expert_down,
            experts_all,
            -(-capacity // 16) * 16,
        )
    group = HQ // KVH
    scale = 1.0 / math.sqrt(HD)
    member = block_ids[None, :] == jnp.arange(NB, dtype=jnp.int32)[:, None]
    count = jnp.sum(member.astype(jnp.float32), axis=-1)
    indicator = member.astype(jnp.bfloat16)
    kmean = jnp.dot(indicator, keys, preferred_element_type=jnp.float32) / count[:, None]
    vmean = jnp.dot(indicator, values, preferred_element_type=jnp.float32) / count[:, None]
    summary_keys = (
        (normalize(kmean.reshape(NB, KVH, HD)) * summary_gain)
        .astype(jnp.bfloat16)
        .reshape(NB, KVH * HD)
    )
    summary_values = (
        normalize(vmean.reshape(NB, KVH, HD)).astype(jnp.bfloat16).reshape(NB, KVH * HD)
    )
    summaries = lax.all_gather(
        jnp.concatenate([summary_keys, summary_values], axis=1), "ctx", axis=0, tiled=True
    )
    all_keys, all_values = summaries[:, : KVH * HD], summaries[:, KVH * HD :]
    index = lax.axis_index("ctx")
    query = queries.reshape(tokens_here, KVH, group, HD)
    key_loc = keys.reshape(tokens_here, KVH, HD)
    remote_keys = all_keys.reshape(-1, KVH, HD)
    causal = jnp.arange(tokens_here)[:, None] >= jnp.arange(tokens_here)[None, :]
    owner = jnp.arange(remote_keys.shape[0], dtype=jnp.int32) // NB
    local = jnp.einsum("tkgd,skd->kgts", query, key_loc, preferred_element_type=jnp.float32) * scale
    local = jnp.where(causal[None, None], local, -jnp.inf)
    remote = (
        jnp.einsum("tkgd,skd->kgts", query, remote_keys, preferred_element_type=jnp.float32) * scale
    )
    remote = jnp.where((owner < index)[None, None, None, :], remote, -jnp.inf)
    scores = jnp.concatenate([local, remote], axis=-1)
    top = jnp.max(scores, axis=-1, keepdims=True)
    expo = jnp.exp(scores - top)
    weights = (expo / jnp.sum(expo, axis=-1, keepdims=True)).astype(jnp.bfloat16)
    every_value = jnp.concatenate(
        [values.reshape(tokens_here, KVH, HD), all_values.reshape(-1, KVH, HD)], axis=0
    )
    attended = jnp.einsum(
        "kgts,skd->tkgd", weights, every_value, preferred_element_type=jnp.float32
    )
    attended = attended.reshape(tokens_here, HQ * HD).astype(jnp.bfloat16)
    hidden = jnp.dot(
        attended,
        lax.all_gather(out_weight, "ctx", axis=0, tiled=True),
        preferred_element_type=jnp.float32,
    )
    normed = (normalize(hidden) * norm_gain).astype(jnp.bfloat16)
    flat_routes = routes.reshape(-1)
    hits = (flat_routes[:, None] == jnp.arange(experts_all, dtype=jnp.int32)[None, :]).astype(
        jnp.int32
    )
    slot = jnp.sum(hits * (jnp.cumsum(hits, axis=0) - 1), axis=-1)
    target = flat_routes * capacity + slot
    source = jnp.arange(tokens_here * TOP, dtype=jnp.int32) // TOP
    outgoing = jnp.zeros((experts_all * capacity, D), jnp.bfloat16).at[target].set(normed[source])
    outgoing = outgoing.reshape(experts_all, capacity, D)
    arrived = lax.all_to_all(outgoing, "ctx", split_axis=0, concat_axis=0, tiled=True)
    senders = arrived.shape[0] // EXP_DEV
    width = arrived.shape[1]
    inputs = (
        arrived.reshape(senders, EXP_DEV, width, D)
        .transpose(1, 0, 2, 3)
        .reshape(EXP_DEV, senders * width, D)
    )
    gate = jnp.einsum("erd,edf->erf", inputs, expert_gate, preferred_element_type=jnp.float32)
    upper = jnp.einsum("erd,edf->erf", inputs, expert_up, preferred_element_type=jnp.float32)
    act = (jax.nn.silu(gate) * upper).astype(jnp.bfloat16)
    result = jnp.einsum(
        "erf,efd->erd", act, expert_down, preferred_element_type=jnp.float32
    ).astype(jnp.bfloat16)
    result = (
        result.reshape(EXP_DEV, senders, width, D)
        .transpose(1, 0, 2, 3)
        .reshape(senders * EXP_DEV, width, D)
    )
    returned = lax.all_to_all(result, "ctx", split_axis=0, concat_axis=0, tiled=True)
    returned = returned.reshape(experts_all * capacity, D)
    picked = jnp.take(returned, target, axis=0).reshape(tokens_here, TOP, D)
    blended = jnp.sum(combine[:, :, None] * picked.astype(jnp.float32), axis=1)
    return (hidden.astype(jnp.bfloat16), (hidden + blended).astype(jnp.bfloat16))


def solution(mesh):
    in_specs = (
        P(("groups", "ctx"), None),
        P(("groups", "ctx"), None),
        P(("groups", "ctx"), None),
        P(("groups", "ctx")),
        P("ctx", None),
        P(),
        P(),
        P(("groups", "ctx"), None),
        P(("groups", "ctx"), None),
        P("ctx", None, None),
        P("ctx", None, None),
        P("ctx", None, None),
    )
    out_specs = (P(("groups", "ctx"), None), P(("groups", "ctx"), None))
    return jax.shard_map(body, mesh=mesh, in_specs=in_specs, out_specs=out_specs, check_vma=False)
```

```python
import functools
import math

import jax
import jax.numpy as jnp
from jax import lax
from jax.experimental import pallas as pl
from jax.experimental.pallas import tpu as pltpu
from jax.sharding import PartitionSpec as P

D = 2048
HQ = 16
KVH = 4
HD = 128
TOP = 8
EXP_DEV = 1
NB = 4


def normalize(x):
    return x * lax.rsqrt(jnp.mean(x * x, axis=-1, keepdims=True) + 1e-06)


RING_BYTES = 16 * 2**20
PASSES = 2
PARTS = 2


def chip_at(position, chips):
    depth = chips // 2
    y = position // depth
    return (position * (1 - y) + (chips - 1 - position) * y) * 2 + y


def layer_kernel(
    n,
    cap,
    queries,
    keys,
    values,
    blocks,
    weight_own,
    key_gain,
    norm_gain,
    routes,
    route_scores,
    gate_hbm,
    up_hbm,
    down_hbm,
    projected,
    out,
    normed,
    hidden,
    att,
    wq,
    outq,
    hidq,
    sums_own,
    sums,
    share,
    gate_w,
    up_w,
    down_w,
    tok,
    wbuf,
    slots,
    rows_in,
    act,
    place,
    comb,
    results,
    theirs,
    ring_in,
    load_sem,
    s_send,
    s_recv,
    wg_send,
    wg_recv,
    wp_send,
    wp_recv,
    at_send,
    at_recv,
    h_send,
    h_recv,
    w_send,
    w_recv,
    ag_send,
    ag_recv,
    pt_send,
    pt_recv,
    y_send,
    y_recv,
    rs_send_sem,
    rs_recv_sem,
):
    tokens = normed.shape[0]
    half = tokens // 2
    width = normed.shape[1]
    ff = gate_w.shape[1]
    chips = n // 2
    far = chips // 2
    me = lax.axis_index("ctx")
    core = me % 2
    y = (me // 2) % 2
    z = me // 4
    pos = z * (1 - y) + (chips - 1 - z) * y
    partner = me + 1 - 2 * core
    ahead = chip_at((pos + 1) % chips, chips) * 2 + core
    behind = chip_at((pos + chips - 1) % chips, chips) * 2 + core
    neighbour = (ahead, behind)

    loads = [
        pltpu.make_async_copy(a, b, load_sem.at[k])
        for k, (a, b) in enumerate(((gate_hbm, gate_w), (up_hbm, up_w), (down_hbm, down_w)))
    ]
    for load in loads:
        load.start()

    barrier = pltpu.get_barrier_semaphore()
    across = 1 - lax.axis_index("groups")

    def greet(k, _):
        pl.semaphore_signal(barrier, inc=1, device_id={"ctx": (me + k) % n})
        return 0

    lax.fori_loop(1, n, greet, 0)
    pl.semaphore_signal(barrier, inc=1, device_id={"groups": across})
    pl.semaphore_signal(barrier, inc=1, device_id={"groups": across, "ctx": partner})

    def mean_of(ref):
        shape = (2 * NB, tokens)
        ids = jnp.broadcast_to(blocks[...], shape)
        member = jnp.where(ids == lax.broadcasted_iota(jnp.int32, shape, 0) % NB, 1.0, 0.0)
        count = jnp.sum(member, axis=1, keepdims=True)
        return (
            jnp.dot(member.astype(jnp.bfloat16), ref[...], preferred_element_type=jnp.float32)
            / count
        )

    kmean, vmean = mean_of(keys), mean_of(values)
    upper = lax.broadcasted_iota(jnp.int32, (2 * NB, HD), 0) < NB
    for g in range(KVH):
        cols = slice(g * HD, (g + 1) * HD)
        sums_own[:, cols] = jnp.where(
            upper, normalize(kmean[:, cols]) * key_gain[...], normalize(vmean[:, cols])
        ).astype(jnp.bfloat16)
    pl.semaphore_wait(barrier, n + 1)

    def s_copy(k):
        return pltpu.make_async_remote_copy(
            src_ref=sums_own,
            dst_ref=sums.at[me],
            send_sem=s_send.at[k],
            recv_sem=s_recv.at[k],
            device_id={"ctx": (me + 2 * k) % n},
        )

    def sp_copy(k):
        source = (me + n - 2 * k) % n
        return pltpu.make_async_remote_copy(
            src_ref=sums.at[source],
            dst_ref=sums.at[source],
            send_sem=s_send.at[chips + k],
            recv_sem=s_recv.at[chips + k],
            device_id={"ctx": partner},
        )

    own_copy = pltpu.make_async_remote_copy(
        src_ref=sums_own,
        dst_ref=sums.at[me],
        send_sem=s_send.at[chips],
        recv_sem=s_recv.at[chips],
        device_id={"ctx": partner},
    )

    def s_start(k, _):
        s_copy(k).start()
        return 0

    def s_pass(k, _):
        s_copy(k).wait_recv()
        sp_copy(k).start()
        return 0

    def s_wait(k, _):
        sp_copy(k).wait_recv()
        s_copy(k).wait_send()
        sp_copy(k).wait_send()
        return 0

    lax.fori_loop(1, chips, s_start, 0)
    own_copy.start()
    sums[me] = sums_own[...]

    def rows(h):
        return pl.ds(h * half, half)

    def chip(offset):
        return (pos + offset + chips) % chips

    def ag_copy(d, step, h):
        sign = 1 - 2 * d
        q = chip(-sign * (step - 1))
        src = normed.at[rows(h)] if step == 1 else tok.at[q, core, rows(h)]
        return pltpu.make_async_remote_copy(
            src_ref=src,
            dst_ref=tok.at[q, core, rows(h)],
            send_sem=ag_send.at[d, step - 1, h],
            recv_sem=ag_recv.at[d, step - 1, h],
            device_id={"ctx": neighbour[d]},
        )

    def pt_copy(offset, h):
        q = chip(offset)
        src = normed.at[rows(h)] if offset == 0 else tok.at[q, core, rows(h)]
        return pltpu.make_async_remote_copy(
            src_ref=src,
            dst_ref=tok.at[q, core, rows(h)],
            send_sem=pt_send.at[offset % chips, h],
            recv_sem=pt_recv.at[offset % chips, h],
            device_id={"ctx": partner},
        )

    def order(d):
        return (0, 1) if d == 0 else (1, 0)

    wrows = weight_own.shape[0]
    passes, pcols = wq.shape[0], wq.shape[3]
    group = 1 - across
    slot = group * 2 + core

    def own_rows(t):
        return pl.ds(pl.multiple_of((core if t == 0 else 1 - core) * wrows, wrows), wrows)

    def w_cols(t, p):
        side = group * 2 + (core if t == 0 else 1 - core)
        return pl.ds(pl.multiple_of((side * passes + p) * pcols, pcols), pcols)

    def w_at(p, q, t):
        return wq.at[p, chip_at(q, chips), own_rows(t)]

    def wg_copy(d, step, p, t):
        sign = 1 - 2 * d
        if step == 1:
            src, dst = weight_own.at[:, w_cols(t, p)], w_at(p, pos, 0)
            target = neighbour[d] + t * (1 - 2 * core)
        else:
            src = dst = w_at(p, chip(-sign * (step - 1)), t)
            target = neighbour[d]
        return pltpu.make_async_remote_copy(
            src_ref=src,
            dst_ref=dst,
            send_sem=wg_send.at[d, step - 1, p, t],
            recv_sem=wg_recv.at[d, step - 1, p, t],
            device_id={"ctx": target},
        )

    def wp_copy(p):
        return pltpu.make_async_remote_copy(
            src_ref=weight_own.at[:, w_cols(1, p)],
            dst_ref=w_at(p, pos, 0),
            send_sem=wp_send.at[p],
            recv_sem=wp_recv.at[p],
            device_id={"ctx": partner},
        )

    def at_copy(kind, g):
        span = HQ // KVH * HD
        source = slot if kind < 2 else across * 2 + core
        block = att.at[
            pl.ds(pl.multiple_of(source * tokens, tokens), tokens), g * span : (g + 1) * span
        ]
        return pltpu.make_async_remote_copy(
            src_ref=block,
            dst_ref=block,
            send_sem=at_send.at[kind, g],
            recv_sem=at_recv.at[kind, g],
            device_id={"groups": across} if kind == 1 else {"ctx": partner},
        )

    def h_copy(kind, p):
        target = (
            {"ctx": partner},
            {"groups": across},
            {"groups": across, "ctx": partner},
        )[kind]
        theirs_slot = (group, across, across)[kind] * 2 + (1 - core, core, 1 - core)[kind]
        return pltpu.make_async_remote_copy(
            src_ref=outq.at[p, theirs_slot],
            dst_ref=hidq.at[slot, p],
            send_sem=h_send.at[kind, p],
            recv_sem=h_recv.at[kind, p],
            device_id=target,
        )

    for p in range(passes):
        for k in range(2):
            for d in range(2):
                wg_copy(d, 1, p, order(d)[k]).start()
    for p in range(passes):
        wp_copy(p).start()
        wq[p, chip_at(pos, chips), own_rows(0)] = weight_own[:, w_cols(0, p)]

    def w_copy(k):
        target = (me + k) % n
        return pltpu.make_async_remote_copy(
            src_ref=share.at[target],
            dst_ref=wbuf.at[pos * 2 + core],
            send_sem=w_send.at[k],
            recv_sem=w_recv.at[k],
            device_id={"ctx": target},
        )

    def w_start(k, _):
        w_copy(k).start()
        return 0

    def w_wait(k, _):
        w_copy(k).wait()
        return 0

    chosen_scores = route_scores[...]
    combine = chosen_scores / jnp.sum(chosen_scores, axis=0, keepdims=True)
    expert = lax.broadcasted_iota(jnp.int32, (n, tokens), 0)
    table_of = jnp.zeros((n, tokens), jnp.float32)
    for c in range(TOP):
        table_of = table_of + jnp.where(routes[c : c + 1] == expert, combine[c : c + 1], 0.0)
    for e in range(n):
        share[e] = table_of[e : e + 1]
    lax.fori_loop(1, n, w_start, 0)
    wbuf[pos * 2 + core] = share[me]
    lax.fori_loop(1, chips, s_pass, 0)
    own_copy.wait()
    lax.fori_loop(1, chips, s_wait, 0)

    many = HQ // KVH
    scale = 1.0 / math.sqrt(HD)
    tall = (many * tokens, tokens)
    causal = lax.broadcasted_iota(jnp.int32, tall, 0) % tokens >= lax.broadcasted_iota(
        jnp.int32, tall, 1
    )
    far_shape = (many * tokens, n * 2 * NB)
    entry = lax.broadcasted_iota(jnp.int32, far_shape, 1)
    seen = (entry % (2 * NB) < NB) & (entry // (2 * NB) < me)
    contract_last = (((1,), (1,)), ((), ()))

    def attend(g):
        cols = slice(g * HD, (g + 1) * HD)
        heads = [slice((g * many + i) * HD, (g * many + i + 1) * HD) for i in range(many)]
        q = jnp.concatenate([queries[:, c] for c in heads], axis=0)
        table = sums[:, :, cols].astype(jnp.float32).reshape(n * 2 * NB, HD)
        shifted = jnp.concatenate([table[NB:], table[:NB]], axis=0).astype(jnp.bfloat16)
        table = table.astype(jnp.bfloat16)
        near = (
            lax.dot_general(q, keys[:, cols], contract_last, preferred_element_type=jnp.float32)
            * scale
        )
        near = jnp.where(causal, near, -jnp.inf)
        remote = lax.dot_general(q, table, contract_last, preferred_element_type=jnp.float32) * scale
        remote = jnp.where(seen, remote, -jnp.inf)
        top = jnp.maximum(
            jnp.max(near, axis=1, keepdims=True), jnp.max(remote, axis=1, keepdims=True)
        )
        near, remote = jnp.exp(near - top), jnp.exp(remote - top)
        total = jnp.sum(near, axis=1, keepdims=True) + jnp.sum(remote, axis=1, keepdims=True)
        near, remote = (near / total).astype(jnp.bfloat16), (remote / total).astype(jnp.bfloat16)
        result = jnp.dot(
            near, values[:, cols], preferred_element_type=jnp.float32
        ) + jnp.dot(remote, shifted, preferred_element_type=jnp.float32)
        result = result.astype(jnp.bfloat16)
        for i, c in enumerate(heads):
            att[pl.ds(pl.multiple_of(slot * tokens, tokens), tokens), c] = result[
                i * tokens : (i + 1) * tokens
            ]
        at_copy(1, g).start()
        at_copy(0, g).start()

    def project(p):
        weight = wq[p].reshape(chips * 2 * wrows, pcols)
        for side in (across, group):
            left = att[pl.ds(pl.multiple_of(side * 2 * tokens, 2 * tokens), 2 * tokens)]
            part = jnp.dot(left, weight, preferred_element_type=jnp.float32).astype(jnp.bfloat16)
            for c in range(2):
                outq[p, side * 2 + c] = part[c * tokens : (c + 1) * tokens]
            if side is across:
                h_copy(1, p).start()
                h_copy(2, p).start()
            else:
                h_copy(0, p).start()
        hidq[slot, p] = outq[p, slot]

    def w_step(step, p):
        for k in range(2):
            for d in range(2):
                t = order(d)[k]
                if step < far or k == 0:
                    wg_copy(d, step, p, t).wait_recv()
                if step + 1 < far or (step + 1 == far and k == 0):
                    wg_copy(d, step + 1, p, t).start()

    def hand_on(g):
        at_copy(1, g).wait_recv()
        at_copy(2, g).start()

    hops = [(step, p) for step in range(1, far) for p in range(passes)]
    w_step(*hops.pop(0))
    for g in range(KVH):
        attend(g)
        if g > 1:
            hand_on(g - 2)
        if g + 1 < KVH:
            w_step(*hops.pop(0))
    for hop in hops:
        w_step(*hop)
    for g in range(KVH - 2, KVH):
        hand_on(g)
    for p in range(passes):
        wp_copy(p).wait_recv()
    for g in range(KVH):
        at_copy(0, g).wait_recv()
        at_copy(2, g).wait_recv()
    for p in range(passes):
        w_step(far, p)
        project(p)
    square = jnp.zeros((tokens, 1), jnp.float32)
    for p in range(passes):
        for kind in range(3):
            h_copy(kind, p).wait_recv()
        for s in range(4):
            at = (s * passes + p) * pcols
            block = hidq[s, p].astype(jnp.float32)
            hidden[:, at : at + pcols] = block
            square = square + jnp.sum(block * block, axis=1, keepdims=True)
    inverse = lax.rsqrt(square / width + 1e-06)
    for h in range(2):
        tidy = hidden[rows(h)] * inverse[h * half : (h + 1) * half] * norm_gain[...]
        normed[rows(h)] = tidy.astype(jnp.bfloat16)
        ag_copy(h, 1, h).start()
    for d in range(2):
        ag_copy(d, 1, 1 - d).start()
    for h in range(2):
        pt_copy(0, h).start()
    projected[...] = hidden[...].astype(jnp.bfloat16)
    tok[pos, core] = normed[...]

    def prepare():
        lax.fori_loop(1, n, w_wait, 0)
        weight = wbuf[...].reshape(n, tokens)
        earlier = lax.broadcasted_iota(jnp.int32, (tokens, tokens), 0) < lax.broadcasted_iota(
            jnp.int32, (tokens, tokens), 1
        )
        earlier = jnp.where(earlier, 1.0, 0.0).astype(jnp.bfloat16)
        chosen = jnp.where(weight > 0.0, 1.0, 0.0).astype(jnp.bfloat16)
        slot_of = jnp.dot(chosen, earlier, preferred_element_type=jnp.float32)
        slot_of = jnp.where(weight > 0.0, slot_of, -1.0)
        for e in range(n):
            slots[e] = slot_of[e : e + 1]
        place[...] = jnp.zeros_like(place)
        for load in loads:
            load.wait()

    part_width = width // PARTS

    def cols_of(c):
        return slice(c * part_width, (c + 1) * part_width)

    def y_copy(offset, c):
        q = chip(offset)
        return pltpu.make_async_remote_copy(
            src_ref=results.at[q, 1 - core, :, cols_of(c)],
            dst_ref=theirs.at[q, :, cols_of(c)],
            send_sem=y_send.at[offset % chips, c],
            recv_sem=y_recv.at[offset % chips, c],
            device_id={"ctx": partner},
        )

    def gather(offsets):
        line = lax.broadcasted_iota(jnp.int32, (cap, tokens), 0).astype(jnp.float32)
        for i, offset in enumerate(offsets):
            q = chip(offset)
            for side in range(2):
                hit = jnp.broadcast_to(slots[q * 2 + side], (cap, tokens)) == line
                pick = jnp.where(hit, 1.0, 0.0).astype(jnp.bfloat16)
                span = slice(side * cap, (side + 1) * cap)
                place[i, span, side * tokens : (side + 1) * tokens] = pick
                scaled = jnp.where(hit, jnp.broadcast_to(wbuf[q * 2 + side], (cap, tokens)), 0.0)
                comb[i, span] = jnp.broadcast_to(
                    jnp.sum(scaled, axis=1, keepdims=True), (cap, 128)
                )
        for i, offset in enumerate(offsets):
            q = chip(offset)
            for h in range(2):
                pt_copy(offset, h).wait_recv()
            for c in range(0, width, 512):
                rows_in[i * 2 * cap : (i + 1) * 2 * cap, c : c + 512] = jnp.dot(
                    place[i],
                    tok[q, :, :, c : c + 512].reshape(2 * tokens, 512),
                    preferred_element_type=jnp.float32,
                ).astype(jnp.bfloat16)

    def expand(offsets):
        many_rows = len(offsets) * 2 * cap

        def in_tile(k, _):
            cols = pl.ds(pl.multiple_of(k * 256, 256), 256)
            x = rows_in[:many_rows]
            g = jnp.dot(x, gate_w[:, cols], preferred_element_type=jnp.float32)
            u = jnp.dot(x, up_w[:, cols], preferred_element_type=jnp.float32)
            act[:many_rows, cols] = (g / (1.0 + jnp.exp(-g)) * u).astype(jnp.bfloat16)
            return 0

        lax.fori_loop(0, ff // 256, in_tile, 0)

    def finish(offsets):
        many_rows = len(offsets) * 2 * cap
        for c in range(PARTS):
            r = jnp.dot(
                act[:many_rows], down_w[:, cols_of(c)], preferred_element_type=jnp.float32
            )
            r = r.astype(jnp.bfloat16).astype(jnp.float32)
            for i, offset in enumerate(offsets):
                part = r[i * 2 * cap : (i + 1) * 2 * cap] * comb[i][:, 0:1]
                spread = lax.dot_general(
                    place[i],
                    part.astype(jnp.bfloat16),
                    (((0,), (0,)), ((), ())),
                    preferred_element_type=jnp.float32,
                ).astype(jnp.bfloat16)
                for side in range(2):
                    results[chip(offset), side, :, cols_of(c)] = spread[
                        side * tokens : (side + 1) * tokens
                    ]
            for offset in offsets:
                y_copy(offset, c).start()

    def relay(step, k):
        for d in range(2):
            h = order(d)[k]
            sign = 1 - 2 * d
            ag_copy(d, step, h).wait_recv()
            if step + 1 < far or (step + 1 == far and k == 0):
                ag_copy(d, step + 1, h).start()
            pt_copy(-sign * step, h).start()

    relay(1, 0)
    prepare()
    relay(1, 1)
    for step in range(1, far):
        pair = (-step, step)
        gather(pair)
        expand(pair)
        if step + 1 < far:
            relay(step + 1, 0)
        finish(pair)
        if step + 1 < far:
            relay(step + 1, 1)

    def sum_of(q, h, c):
        own = results[q, core, rows(h), cols_of(c)].astype(jnp.float32)
        return own + theirs[q, rows(h), cols_of(c)].astype(jnp.float32)

    def rs_copy(d, step, h, c, src):
        return pltpu.make_async_remote_copy(
            src_ref=src,
            dst_ref=ring_in.at[d, step - 1, h, :, cols_of(c)],
            send_sem=rs_send_sem.at[d, step - 1, h, c],
            recv_sem=rs_recv_sem.at[d, step - 1, h, c],
            device_id={"ctx": neighbour[d]},
        )

    def landed(d, step, h, c):
        return ring_in.at[d, step - 1, h, :, cols_of(c)]

    def rs_part(d, step, k, c):
        h = order(d)[k]
        sign = 1 - 2 * d
        q = chip(sign * (far + 1 - step))
        if step == 1 or (step == 2 and k == 1):
            results[q, core, rows(h), cols_of(c)] = sum_of(q, h, c).astype(jnp.bfloat16)
            src = results.at[q, core, rows(h), cols_of(c)]
        else:
            src = landed(d, step - 1, h, c)
            rs_copy(d, step - 1, h, c, src).wait_recv()
            ring_in[d, step - 2, h, :, cols_of(c)] = (
                ring_in[d, step - 2, h, :, cols_of(c)].astype(jnp.float32) + sum_of(q, h, c)
            ).astype(jnp.bfloat16)
        rs_copy(d, step, h, c, src).start()

    def rs_step(step, k):
        for c in range(PARTS):
            for d in range(2):
                rs_part(d, step, k, c)

    for step in range(1, far - 1):
        for offset in (-step, step):
            for c in range(PARTS):
                y_copy(offset, c).wait_recv()
    for c in range(PARTS):
        for d in range(2):
            y_copy((1 - 2 * d) * (far - 1), c).wait_recv()
            rs_part(d, 2, 1, c)
    relay(far, 0)
    gather((far,))
    expand((far,))
    finish((far,))
    for c in range(PARTS):
        y_copy(far, c).wait_recv()
        for d in range(2):
            rs_part(d, 1, 0, c)
    for step in range(2, far + 1):
        if step < far:
            rs_step(step + 1, 1)
        if step == 2:
            gather((0,))
            expand((0,))
        rs_step(step, 0)
        if step == 2:
            finish((0,))
    for c in range(PARTS):
        y_copy(0, c).wait_recv()
    for c in range(PARTS):
        for h in range(2):
            total = hidden[rows(h), cols_of(c)] + sum_of(pos, h, c)
            for d in range(2):
                rs_copy(d, far, h, c, landed(d, far, h, c)).wait_recv()
                total = total + ring_in[d, far - 1, h, :, cols_of(c)].astype(jnp.float32)
            out[rows(h), cols_of(c)] = total.astype(jnp.bfloat16)

    for d in range(2):
        for step in range(1, far + 1):
            for k in range(2):
                h = order(d)[k]
                if step < far or k == 0:
                    ag_copy(d, step, h).wait_send()
                if step > 1 or k == 0:
                    for c in range(PARTS):
                        rs_copy(d, step, h, c, landed(d, step, h, c)).wait_send()
    for offset in range(chips):
        for h in range(2):
            pt_copy(offset, h).wait_send()
        for c in range(PARTS):
            y_copy(offset, c).wait_send()


    for p in range(passes):
        for d in range(2):
            for step in range(1, far + 1):
                for k in range(2):
                    if step < far or k == 0:
                        wg_copy(d, step, p, order(d)[k]).wait_send()
        wp_copy(p).wait_send()
        for kind in range(3):
            h_copy(kind, p).wait_send()
    for g in range(KVH):
        for kind in range(3):
            at_copy(kind, g).wait_send()


def write_kernel(a, b, a_out, b_out, sem):
    copies = [
        pltpu.make_async_copy(x, y, sem.at[k]) for k, (x, y) in enumerate(((a, a_out), (b, b_out)))
    ]
    for copy in copies:
        copy.start()
    for copy in copies:
        copy.wait()


def layer_ring(
    queries,
    keys,
    values,
    block_ids,
    out_weight,
    summary_gain,
    norm_gain,
    routes,
    route_scores,
    expert_gate,
    expert_up,
    expert_down,
    n,
    cap,
):
    tokens, width = queries.shape
    ff = expert_gate.shape[-1]
    chips = n // 2
    far = chips // 2
    vmem = pl.BlockSpec(memory_space=pltpu.VMEM)
    hbm = pl.BlockSpec(memory_space=pl.ANY)
    dma = pltpu.SemaphoreType.DMA
    bf16, f32 = jnp.bfloat16, jnp.float32
    result = jax.ShapeDtypeStruct((tokens, width), bf16)
    pair = pl.pallas_call(
        functools.partial(layer_kernel, n, cap),
        out_shape=(result, result),
        in_specs=[vmem] * 9 + [hbm] * 3,
        out_specs=(vmem, vmem),
        scratch_shapes=[
            pltpu.VMEM((tokens, width), bf16),
            pltpu.VMEM((tokens, width), f32),
            pltpu.VMEM((4 * tokens, width), bf16),
            pltpu.VMEM((PASSES, chips, 2 * out_weight.shape[0], width // (4 * PASSES)), bf16),
            pltpu.VMEM((PASSES, 4, tokens, width // (4 * PASSES)), bf16),
            pltpu.VMEM((4, PASSES, tokens, width // (4 * PASSES)), bf16),
            pltpu.VMEM((2 * NB, KVH * HD), bf16),
            pltpu.VMEM((n, 2 * NB, KVH * HD), bf16),
            pltpu.VMEM((n, 1, tokens), f32),
            pltpu.VMEM((width, ff), bf16),
            pltpu.VMEM((width, ff), bf16),
            pltpu.VMEM((ff, width), bf16),
            pltpu.VMEM((chips, 2, tokens, width), bf16),
            pltpu.VMEM((n, 1, tokens), f32),
            pltpu.VMEM((n, 1, tokens), f32),
            pltpu.VMEM((4 * cap, width), bf16),
            pltpu.VMEM((4 * cap, ff), bf16),
            pltpu.VMEM((2, 2 * cap, 2 * tokens), bf16),
            pltpu.VMEM((2, 2 * cap, 128), f32),
            pltpu.VMEM((chips, 2, tokens, width), bf16),
            pltpu.VMEM((chips, tokens, width), bf16),
            pltpu.VMEM((2, far, 2, tokens // 2, width), bf16),
            dma((3,)),
            dma((n,)),
            dma((n,)),
            dma((2, far, PASSES, 2)),
            dma((2, far, PASSES, 2)),
            dma((PASSES,)),
            dma((PASSES,)),
            dma((3, KVH)),
            dma((3, KVH)),
            dma((3, PASSES)),
            dma((3, PASSES)),
            dma((n,)),
            dma((n,)),
            dma((2, far, 2)),
            dma((2, far, 2)),
            dma((chips, 2)),
            dma((chips, 2)),
            dma((chips, PARTS)),
            dma((chips, PARTS)),
            dma((2, far, 2, PARTS)),
            dma((2, far, 2, PARTS)),
        ],
        compiler_params=pltpu.CompilerParams(
            collective_id=1, has_side_effects=True, vmem_limit_bytes=62 * 2**20
        ),
    )(
        queries,
        keys,
        values,
        block_ids[None, :],
        out_weight,
        summary_gain[None, :],
        norm_gain[None, :],
        routes.T,
        route_scores.T,
        expert_gate[0],
        expert_up[0],
        expert_down[0],
    )
    return pl.pallas_call(
        write_kernel,
        out_shape=(result, result),
        in_specs=[vmem] * 2,
        out_specs=(hbm, hbm),
        scratch_shapes=[dma((2,))],
    )(*pair)


def body(
    queries,
    keys,
    values,
    block_ids,
    out_weight,
    summary_gain,
    norm_gain,
    routes,
    route_scores,
    expert_gate,
    expert_up,
    expert_down,
):
    tokens_here = queries.shape[0]
    combine = route_scores / jnp.sum(route_scores, axis=-1, keepdims=True)
    experts_all = EXP_DEV * lax.axis_size("ctx")
    capacity = max(2, 5 * tokens_here * TOP // (4 * experts_all))
    chips = experts_all // 2
    fits = experts_all * tokens_here * D * 2 <= RING_BYTES
    if fits and chips % 4 == 0 and lax.axis_size("groups") == 2:
        return layer_ring(
            queries,
            keys,
            values,
            block_ids,
            out_weight,
            summary_gain,
            norm_gain,
            routes,
            route_scores,
            expert_gate,
            expert_up,
            expert_down,
            experts_all,
            -(-capacity // 16) * 16,
        )
    group = HQ // KVH
    scale = 1.0 / math.sqrt(HD)
    member = block_ids[None, :] == jnp.arange(NB, dtype=jnp.int32)[:, None]
    count = jnp.sum(member.astype(jnp.float32), axis=-1)
    indicator = member.astype(jnp.bfloat16)
    kmean = jnp.dot(indicator, keys, preferred_element_type=jnp.float32) / count[:, None]
    vmean = jnp.dot(indicator, values, preferred_element_type=jnp.float32) / count[:, None]
    summary_keys = (
        (normalize(kmean.reshape(NB, KVH, HD)) * summary_gain)
        .astype(jnp.bfloat16)
        .reshape(NB, KVH * HD)
    )
    summary_values = (
        normalize(vmean.reshape(NB, KVH, HD)).astype(jnp.bfloat16).reshape(NB, KVH * HD)
    )
    summaries = lax.all_gather(
        jnp.concatenate([summary_keys, summary_values], axis=1), "ctx", axis=0, tiled=True
    )
    all_keys, all_values = summaries[:, : KVH * HD], summaries[:, KVH * HD :]
    index = lax.axis_index("ctx")
    query = queries.reshape(tokens_here, KVH, group, HD)
    key_loc = keys.reshape(tokens_here, KVH, HD)
    remote_keys = all_keys.reshape(-1, KVH, HD)
    causal = jnp.arange(tokens_here)[:, None] >= jnp.arange(tokens_here)[None, :]
    owner = jnp.arange(remote_keys.shape[0], dtype=jnp.int32) // NB
    local = jnp.einsum("tkgd,skd->kgts", query, key_loc, preferred_element_type=jnp.float32) * scale
    local = jnp.where(causal[None, None], local, -jnp.inf)
    remote = (
        jnp.einsum("tkgd,skd->kgts", query, remote_keys, preferred_element_type=jnp.float32) * scale
    )
    remote = jnp.where((owner < index)[None, None, None, :], remote, -jnp.inf)
    scores = jnp.concatenate([local, remote], axis=-1)
    top = jnp.max(scores, axis=-1, keepdims=True)
    expo = jnp.exp(scores - top)
    weights = (expo / jnp.sum(expo, axis=-1, keepdims=True)).astype(jnp.bfloat16)
    every_value = jnp.concatenate(
        [values.reshape(tokens_here, KVH, HD), all_values.reshape(-1, KVH, HD)], axis=0
    )
    attended = jnp.einsum(
        "kgts,skd->tkgd", weights, every_value, preferred_element_type=jnp.float32
    )
    attended = attended.reshape(tokens_here, HQ * HD).astype(jnp.bfloat16)
    hidden = jnp.dot(
        attended,
        lax.all_gather(out_weight, "ctx", axis=0, tiled=True),
        preferred_element_type=jnp.float32,
    )
    normed = (normalize(hidden) * norm_gain).astype(jnp.bfloat16)
    flat_routes = routes.reshape(-1)
    hits = (flat_routes[:, None] == jnp.arange(experts_all, dtype=jnp.int32)[None, :]).astype(
        jnp.int32
    )
    slot = jnp.sum(hits * (jnp.cumsum(hits, axis=0) - 1), axis=-1)
    target = flat_routes * capacity + slot
    source = jnp.arange(tokens_here * TOP, dtype=jnp.int32) // TOP
    outgoing = jnp.zeros((experts_all * capacity, D), jnp.bfloat16).at[target].set(normed[source])
    outgoing = outgoing.reshape(experts_all, capacity, D)
    arrived = lax.all_to_all(outgoing, "ctx", split_axis=0, concat_axis=0, tiled=True)
    senders = arrived.shape[0] // EXP_DEV
    width = arrived.shape[1]
    inputs = (
        arrived.reshape(senders, EXP_DEV, width, D)
        .transpose(1, 0, 2, 3)
        .reshape(EXP_DEV, senders * width, D)
    )
    gate = jnp.einsum("erd,edf->erf", inputs, expert_gate, preferred_element_type=jnp.float32)
    upper = jnp.einsum("erd,edf->erf", inputs, expert_up, preferred_element_type=jnp.float32)
    act = (jax.nn.silu(gate) * upper).astype(jnp.bfloat16)
    result = jnp.einsum(
        "erf,efd->erd", act, expert_down, preferred_element_type=jnp.float32
    ).astype(jnp.bfloat16)
    result = (
        result.reshape(EXP_DEV, senders, width, D)
        .transpose(1, 0, 2, 3)
        .reshape(senders * EXP_DEV, width, D)
    )
    returned = lax.all_to_all(result, "ctx", split_axis=0, concat_axis=0, tiled=True)
    returned = returned.reshape(experts_all * capacity, D)
    picked = jnp.take(returned, target, axis=0).reshape(tokens_here, TOP, D)
    blended = jnp.sum(combine[:, :, None] * picked.astype(jnp.float32), axis=1)
    return (hidden.astype(jnp.bfloat16), (hidden + blended).astype(jnp.bfloat16))


def solution(mesh):
    in_specs = (
        P(("groups", "ctx"), None),
        P(("groups", "ctx"), None),
        P(("groups", "ctx"), None),
        P(("groups", "ctx")),
        P("ctx", None),
        P(),
        P(),
        P(("groups", "ctx"), None),
        P(("groups", "ctx"), None),
        P("ctx", None, None),
        P("ctx", None, None),
        P("ctx", None, None),
    )
    out_specs = (P(("groups", "ctx"), None), P(("groups", "ctx"), None))
    return jax.shard_map(body, mesh=mesh, in_specs=in_specs, out_specs=out_specs, check_vma=False)
```
